32 devices in a mesh: groups: 2 (over y), gx: 16 (over z, x, core).
Axes of the slice: x: 2, y: 2, z: 4, core: 2. Of those that a mesh axis runs over, the one named last changes fastest.
Arguments:
- features: float32 [48, 64, 96, 128], P(None, ('groups', 'gx')), parts along dimension 1, may hold values from -6 to 6
- fine_weights: bfloat16 [1536, 8, 48, 48], P('gx'), may hold values from -1.796875 to 1.796875
- middle_weights: bfloat16 [384, 4, 48, 48], P('gx'), may hold values from -3 to 3
- lift_fine: float32 [48, 48], replicated, may hold values from -0.875 to 0.875
- lift_middle: float32 [48, 48], replicated, may hold values from -0.875 to 0.875
- project_out: float32 [48, 48], replicated, may hold values from -0.875 to 0.875
Outputs:
- result: float32 [48, 64, 96, 128], P(None, ('groups', 'gx')), parts along dimension 1
The draws below stay inside these ranges and needn't reach their ends.
There are 2 independent parts, one for each index of `groups`. The reference program is written for one: setup_inputs(seed, part) draws one part's arguments, and reference() takes and returns one part's arrays. A program takes and returns all parts, laid end to end along the dimension named above; an argument that names none is the same for every part. Nothing has to cross between parts.
All inputs are finite; a program needn't handle non-finite values.
Results may differ from the reference program's by a relative error of at most 0.0018.
Values sent between devices are 32-bit elements; how exact they have to be, the bound alone decides.
A program may use at most 128 MiB of HBM per device.

```python
import jax
import jax.numpy as jnp
from jax import lax

C = 48
NY = 96
NZ = 128
KY = 48
KZ = 32
NX = 32
KX = 8
KX2 = 4
MODES = 1536
MODES2 = 384


def levels(own_key, dims, split, smallest, top_value):
    loudness = 1.0
    for dim, parts in split:
        steps = jax.random.uniform(jax.random.fold_in(jax.random.fold_in(own_key, 6), dim), (parts,), jnp.float32, smallest / len(split), top_value / len(split))
        loudness = loudness * jnp.repeat(jnp.exp(steps), dims[dim] // parts).reshape((-1,) + (1,) * (len(dims) - 1 - dim))
    return loudness


def normal_values(own_key, dims, scale, limit, split=(), kind=jnp.bfloat16):
    drawn = scale * jax.random.normal(own_key, dims, jnp.float32)
    if split:
        drawn = drawn * levels(own_key, dims, split, -0.22, 0.18)
    return jnp.clip(drawn, -limit, limit).astype(kind)


def setup_inputs(seed: int = 0, part: int = 0) -> dict:
    streams_of = jax.random.split(jax.random.key(seed), 7)
    part_keys = jax.random.split(jax.random.fold_in(streams_of[6], part), 7)
    features = normal_values(part_keys[0], (C, NX, NY, NZ), 1.0, 6.0, ((1, 16),), jnp.float32)
    fine_weights = normal_values(streams_of[1], (MODES, KX, C, C), 0.3, 1.796875, ((0, 16),))
    middle_weights = normal_values(streams_of[2], (MODES2, KX2, C, C), 0.5, 3.0, ((0, 16),))
    lift_fine = normal_values(streams_of[3], (C, C), C ** -0.5, 0.875, (), jnp.float32)
    lift_middle = normal_values(streams_of[4], (C, C), C ** -0.5, 0.875, (), jnp.float32)
    project_out = normal_values(streams_of[5], (C, C), C ** -0.5, 0.875, (), jnp.float32)
    return dict(features=features, fine_weights=fine_weights, middle_weights=middle_weights, lift_fine=lift_fine, lift_middle=lift_middle, project_out=project_out)


HIGHEST = lax.Precision.HIGHEST

def cosine_table(modes_kept, length, offset, columns):
    orders = jnp.arange(modes_kept, dtype=jnp.int32)[:, None]
    points = offset + jnp.arange(columns, dtype=jnp.int32)[None, :]
    phase = orders * (2 * points + 1) % (4 * length)
    angle = jnp.pi / (2 * length) * phase.astype(jnp.float32)
    scales = jnp.where(orders == 0, jnp.sqrt(jnp.float32(1.0 / length)), jnp.sqrt(jnp.float32(2.0 / length)))
    return scales.astype(jnp.float32) * jnp.cos(angle)

def forward_yz(values, modes_y, modes_z):
    channels, local_x, cells_y, cells_z = values.shape
    table_z = cosine_table(modes_z, cells_z, 0, cells_z)
    table_y = cosine_table(modes_y, cells_y, 0, cells_y)
    along_z = jnp.einsum('cxyz,jz->cxyj', values, table_z, precision=HIGHEST)
    both = jnp.einsum('cxyj,iy->ijxc', along_z, table_y, precision=HIGHEST)
    return both.reshape(modes_y * modes_z, local_x, channels)

def inverse_yz(coeffs, modes_y, modes_z, cells_y, cells_z):
    total, local_x, channels = coeffs.shape
    shaped = coeffs.reshape(modes_y, modes_z, local_x, channels)
    table_z = cosine_table(modes_z, cells_z, 0, cells_z)
    table_y = cosine_table(modes_y, cells_y, 0, cells_y)
    along_y = jnp.einsum('ijxc,iy->jxcy', shaped, table_y, precision=HIGHEST)
    return jnp.einsum('jxcy,jz->cxyz', along_y, table_z, precision=HIGHEST)

def spectral(values, weights, modes_x, modes_y, modes_z):
    channels, cells_x, cells_y, cells_z = values.shape
    coeffs = forward_yz(values, modes_y, modes_z)
    table_x = cosine_table(modes_x, cells_x, 0, cells_x)
    modal = jnp.einsum('mxc,kx->mkc', coeffs, table_x, precision=HIGHEST)
    modal_b = modal.astype(jnp.bfloat16)
    mixed = jnp.einsum('mkc,mkco->mko', modal_b.astype(jnp.float32), weights.astype(jnp.float32), precision=HIGHEST)
    back = jnp.einsum('mkc,kx->mxc', mixed, table_x, precision=HIGHEST)
    return inverse_yz(back, modes_y, modes_z, cells_y, cells_z)

def pointwise(values, matrix):
    return jnp.einsum('cxyz,co->oxyz', values, matrix, precision=HIGHEST)

def coarsen(values):
    channels, cells_x, cells_y, cells_z = values.shape
    shaped = values.reshape(channels, cells_x // 2, 2, cells_y // 2, 2, cells_z // 2, 2)
    return lax.optimization_barrier(jnp.mean(shaped, axis=(2, 4, 6)))

def refine(values):
    return jnp.repeat(jnp.repeat(jnp.repeat(values, 2, axis=1), 2, axis=2), 2, axis=3)

def reference(features, fine_weights, middle_weights, lift_fine, lift_middle, project_out):
    level_one = jax.nn.gelu(spectral(features, fine_weights, KX, KY, KZ) + pointwise(features, lift_fine), approximate=False)
    pooled = coarsen(level_one)
    level_two = jax.nn.gelu(spectral(pooled, middle_weights, KX2, KY // 2, KZ // 2) + pointwise(pooled, lift_middle), approximate=False)
    return features + pointwise(level_one + refine(level_two), project_out)
```

```python
import functools

import jax
import jax.numpy as jnp
import numpy as np
from jax import lax
from jax.experimental import pallas as pl
from jax.experimental.pallas import tpu as pltpu
from jax.sharding import PartitionSpec as P

KY = 48
KZ = 32


HIGHEST = lax.Precision.HIGHEST


def cosine_table(modes_kept, length, columns):
    orders = jnp.arange(modes_kept, dtype=jnp.int32)[:, None]
    points = jnp.arange(columns, dtype=jnp.int32)[None, :]
    phase = orders * (2 * points + 1) % (4 * length)
    angle = jnp.pi / (2 * length) * phase.astype(jnp.float32)
    scales = jnp.where(
        orders == 0, jnp.sqrt(jnp.float32(1.0 / length)), jnp.sqrt(jnp.float32(2.0 / length))
    )
    return scales * jnp.cos(angle)


def forward_yz(values, modes_y, modes_z):
    channels, local_x, cells_y, cells_z = values.shape
    table_z = cosine_table(modes_z, cells_z, cells_z)
    table_y = cosine_table(modes_y, cells_y, cells_y)
    along_z = jnp.einsum("cxyz,jz->cxyj", values, table_z, precision=HIGHEST)
    both = jnp.einsum("cxyj,iy->ijxc", along_z, table_y, precision=HIGHEST)
    return both.reshape(modes_y * modes_z, local_x, channels)


def inverse_yz(coeffs, modes_y, modes_z, cells_y, cells_z):
    total, local_x, channels = coeffs.shape
    shaped = coeffs.reshape(modes_y, modes_z, local_x, channels)
    table_z = cosine_table(modes_z, cells_z, cells_z)
    table_y = cosine_table(modes_y, cells_y, cells_y)
    along_y = jnp.einsum("ijxc,iy->jxcy", shaped, table_y, precision=HIGHEST)
    return jnp.einsum("jxcy,jz->cxyz", along_y, table_z, precision=HIGHEST)


def mix_modes(modal, weights):
    return jnp.einsum(
        "mkc,mkco->mko", modal.astype(jnp.bfloat16), weights, preferred_element_type=jnp.float32
    )


def pointwise(values, matrix):
    return jnp.einsum("cxyz,co->oxyz", values, matrix, precision=HIGHEST)


def coarsen(values):
    channels, cells_x, cells_y, cells_z = values.shape
    shaped = values.reshape(channels, cells_x // 2, 2, cells_y // 2, 2, cells_z // 2, 2)
    return jnp.mean(shaped, axis=(2, 4, 6))


def refine(values):
    return jnp.repeat(jnp.repeat(jnp.repeat(values, 2, axis=1), 2, axis=2), 2, axis=3)


def general_device(features, fine_weights, middle_weights, lift_fine, lift_middle, project_out):
    channels, local_x, cells_y, cells_z = features.shape
    group_size = lax.axis_size("gx")
    cells_x = local_x * group_size
    modes_x = fine_weights.shape[1]
    coeffs = forward_yz(features, KY, KZ)
    table_x = cosine_table(modes_x, cells_x, cells_x)
    owned_pairs = coeffs.shape[0] // group_size
    grouped = coeffs.reshape(group_size, owned_pairs, local_x, channels)
    modal = jnp.einsum(
        "amxc,kx->mkc",
        lax.all_to_all(grouped, "gx", split_axis=0, concat_axis=2, tiled=True),
        table_x,
        precision=HIGHEST,
    )
    mixed = mix_modes(modal, fine_weights)
    back = jnp.einsum("mkc,kx->mxc", mixed, table_x, precision=HIGHEST)
    slabs = lax.all_to_all(back, "gx", split_axis=1, concat_axis=0, tiled=True)
    level_one = jax.nn.gelu(
        inverse_yz(slabs, KY, KZ, cells_y, cells_z) + pointwise(features, lift_fine),
        approximate=False,
    )
    pooled = coarsen(level_one)
    half_x = local_x // 2
    half_ky = KY // 2
    half_kz = KZ // 2
    half_modes = middle_weights.shape[1]
    coarse_x = half_x * group_size
    coarse_coeffs = forward_yz(pooled, half_ky, half_kz)
    coarse_pencils = lax.all_to_all(coarse_coeffs, "gx", split_axis=0, concat_axis=1, tiled=True)
    coarse_table = cosine_table(half_modes, coarse_x, coarse_x)
    coarse_modal = jnp.einsum("mxc,kx->mkc", coarse_pencils, coarse_table, precision=HIGHEST)
    coarse_mixed = mix_modes(coarse_modal, middle_weights)
    coarse_back = jnp.einsum("mkc,kx->mxc", coarse_mixed, coarse_table, precision=HIGHEST)
    coarse_slabs = lax.all_to_all(coarse_back, "gx", split_axis=1, concat_axis=0, tiled=True)
    level_two = jax.nn.gelu(
        inverse_yz(coarse_slabs, half_ky, half_kz, cells_y // 2, cells_z // 2)
        + pointwise(pooled, lift_middle),
        approximate=False,
    )
    return features + pointwise(level_one + refine(level_two), project_out)


BF16 = jnp.bfloat16
F32 = jnp.float32


def host_table(modes_kept, length):
    orders = np.arange(modes_kept)[:, None]
    points = np.arange(length)[None, :]
    scales = np.where(orders == 0, np.sqrt(1.0 / length), np.sqrt(2.0 / length))
    return scales * np.cos(np.pi * orders * (2 * points + 1) / (2 * length))


def host_split(table):
    table = np.asarray(table, np.float32)
    high = table.astype(jnp.bfloat16)
    low = (table - high.astype(np.float32)).astype(jnp.bfloat16)
    return high, low


def left_rows(table):
    high, low = host_split(table)
    return jnp.asarray(
        np.concatenate([np.concatenate([high, high], 1), np.concatenate([low, low], 1)], 0)
    )


def left_three(table):
    high, low = host_split(table)
    return jnp.asarray(np.concatenate([high, high, low], 1))


def right_three(table):
    high, low = host_split(table)
    return jnp.asarray(np.concatenate([high, high, low], 0))


def split(values):
    high = values.astype(BF16)
    low = (values - high.astype(F32)).astype(BF16)
    return high, low


def dot(left, right):
    return jnp.dot(left, right, preferred_element_type=F32)


def dot_left3(left3, values):
    high, low = split(values)
    return dot(left3, jnp.concatenate([high, low, high], 0))


def dot_right3(values, right3):
    high, low = split(values)
    return dot(jnp.concatenate([high, low, high], 1), right3)


def gelu(t):
    return 0.5 * t * (1.0 + lax.erf(t * np.float32(np.sqrt(0.5))))


def whole():
    return pl.BlockSpec(memory_space=pltpu.VMEM)


def forward_kernel(rows_per_mode, f_ref, ty_ref, tz_ref, out_ref):
    step = pl.program_id(0)
    per_row, local_x, cells_y, cells_z = f_ref.shape
    modes = ty_ref.shape[0] // 2
    width = 128 // per_row
    lane = lax.broadcasted_iota(jnp.int32, (modes, 128), 1) // width
    total = [jnp.zeros((modes, 128), F32) for _ in range(local_x)]
    for c in range(per_row):
        wide = jnp.concatenate([f_ref[c, x] for x in range(local_x)], 1)
        high, low = split(wide)
        both = dot(ty_ref[...], jnp.concatenate([high, low], 0))
        both = both[:modes] + both[modes:]
        stacked = jnp.concatenate(
            [both[:, x * cells_z : (x + 1) * cells_z] for x in range(local_x)], 0
        )
        done = dot_right3(stacked, tz_ref[...])
        for x in range(local_x):
            total[x] = jnp.where(lane == c, done[x * modes : (x + 1) * modes], total[x])
    chunks = rows_per_mode // local_x
    for x in range(local_x):
        out_ref[pl.ds(x * chunks + step, modes, stride=rows_per_mode), :] = total[x]


def forward_fine(features, modes_y, modes_z):
    channels, local_x, cells_y, cells_z = features.shape
    per_row = 128 // modes_z
    chunks = channels // per_row
    rows = modes_y * local_x * chunks
    ty = left_rows(host_table(modes_y, cells_y))
    tz = right_three(np.tile(host_table(modes_z, cells_z).T, (1, per_row)))
    return pl.pallas_call(
        functools.partial(forward_kernel, local_x * chunks),
        grid=(chunks,),
        out_shape=jax.ShapeDtypeStruct((rows, 128), F32),
        in_specs=[
            pl.BlockSpec((per_row, local_x, cells_y, cells_z), lambda h: (h, 0, 0, 0)),
            pl.BlockSpec(ty.shape, lambda h: (0, 0)),
            pl.BlockSpec(tz.shape, lambda h: (0, 0)),
        ],
        out_specs=pl.BlockSpec((rows, 128), lambda h: (0, 0)),
        name="forward_fine",
    )(features, ty, tz)


def middle_kernel(
    slab_ref, f_ref, ty_ref, tz_ref, lift_ref, proj_ref, yc_ref, zc_ref, zp_ref,
    base_ref, pooled_ref, coarse_ref, spec_ref, sum_ref,
):
    channels, local_x, cells_y, cells_z = f_ref.shape
    modes_y = ty_ref.shape[1] // 3
    rows_per_mode = slab_ref.shape[0] // modes_y
    chunks = rows_per_mode // local_x
    per_row = channels // chunks
    width = 128 // per_row
    lane = lax.broadcasted_iota(jnp.int32, (local_x * cells_y, 128), 1) // width

    def inverse(h, carry):
        wide = jnp.concatenate(
            [slab_ref[pl.ds(x * chunks + h, modes_y, stride=rows_per_mode), :] for x in range(local_x)], 1
        )
        grown = dot_left3(ty_ref[...], wide)
        stacked = jnp.concatenate([grown[:, x * 128 : (x + 1) * 128] for x in range(local_x)], 0)
        high, low = split(stacked)
        left = jnp.concatenate([high, low, high], 1)
        lanes = jnp.concatenate([lane] * 3, 1)
        for c in range(per_row):
            masked = jnp.where(lanes == c, left, jnp.zeros_like(left))
            done = dot(masked, tz_ref[...])
            for x in range(local_x):
                spec_ref[h * per_row + c, x] = done[x * cells_y : (x + 1) * cells_y]
        return carry

    lax.fori_loop(0, chunks, inverse, 0)

    def block(b, carry):
        at = pl.ds(pl.multiple_of(b * 8, 8), 8)
        values = jnp.concatenate(
            [f_ref[:, x, at, :].reshape(channels * 8, cells_z) for x in range(local_x)], 1
        )
        spectral = jnp.concatenate(
            [spec_ref[:, x, at, :].reshape(channels * 8, cells_z) for x in range(local_x)], 1
        )
        level = gelu(dot_left3(lift_ref[...], values) + spectral)
        base = values + dot_left3(proj_ref[...], level)
        for x in range(local_x):
            base_ref[:, x, at, :] = base[:, x * cells_z : (x + 1) * cells_z].reshape(channels, 8, cells_z)
        sum_ref[:, at, :] = (level[:, :cells_z] + level[:, cells_z:]).reshape(channels, 8, cells_z)
        return carry

    lax.fori_loop(0, cells_y // 8, block, 0)

    half_y = cells_y // 2
    modes_c = yc_ref.shape[0] // 2 - half_y
    parts = zc_ref.shape[1] // 128
    coarse_chunks = coarse_ref.shape[0] // (modes_c * parts)
    coarse_per = channels // coarse_chunks
    coarse_lane = (
        lax.broadcasted_iota(jnp.int32, (modes_c, parts * 128), 1) // (128 // coarse_per) % coarse_per
    )
    rows = modes_c + half_y

    def coarse(h, carry):
        total = jnp.zeros((modes_c, parts * 128), F32)
        for pair in range(coarse_per // 2):
            first = h * coarse_per + pair * 2
            wide = jnp.concatenate([sum_ref[first], sum_ref[first + 1]], 1)
            high, low = split(wide)
            both = dot(yc_ref[...], jnp.concatenate([high, low], 0))
            both = both[:rows] + both[rows:]
            modal = jnp.concatenate([both[half_y:, :128], both[half_y:, 128:]], 0)
            done = dot_right3(modal, zc_ref[...])
            for k in range(2):
                total = jnp.where(
                    coarse_lane == pair * 2 + k, done[k * modes_c : (k + 1) * modes_c], total
                )
            flat = jnp.concatenate([both[:half_y, :128], both[:half_y, 128:]], 0)
            high, low = split(flat)
            mean = dot(jnp.concatenate([high, low], 1), zp_ref[...])
            pooled_ref[first] = mean[:half_y]
            pooled_ref[first + 1] = mean[half_y:]
        for p in range(parts):
            coarse_ref[pl.ds(p * coarse_chunks + h, modes_c, stride=parts * coarse_chunks), :] = total[
                :, p * 128 : (p + 1) * 128
            ]
        return carry

    lax.fori_loop(0, coarse_chunks, coarse, 0)


def blockwise(matrix, left):
    high = matrix.astype(BF16)
    low = (matrix - lax.optimization_barrier(high).astype(F32)).astype(BF16)
    out = []
    for part in (high, high, low):
        grown = part.T[:, None, :, None] * jnp.asarray(left, BF16)[None, :, None, :]
        out.append(grown.reshape(matrix.shape[1] * left.shape[0], matrix.shape[0] * left.shape[1]))
    return jnp.concatenate(out, 1)


def final_kernel(
    slab_ref, pooled_ref, base_ref, ty_ref, tz_ref, lift_ref, proj_ref, out_ref, spec_ref
):
    channels, half_y, _ = pooled_ref.shape
    local_x = base_ref.shape[1]
    modes = ty_ref.shape[1] // 3
    rows_per_mode = slab_ref.shape[0] // modes
    parts = tz_ref.shape[0] // (3 * 128)
    chunks = rows_per_mode // parts
    per_row = channels // chunks
    stacked = []
    for h in range(chunks):
        wide = jnp.concatenate(
            [slab_ref[pl.ds(p * chunks + h, modes, stride=rows_per_mode), :] for p in range(parts)], 1
        )
        stacked.append(dot_left3(ty_ref[...], wide))
    grown = jnp.concatenate(stacked, 0)
    high, low = split(grown)
    left = jnp.concatenate([high, low, high], 1)
    lane = lax.broadcasted_iota(jnp.int32, left.shape, 1) // (128 // per_row) % per_row

    for c in range(per_row):
        done = dot(jnp.where(lane == c, left, jnp.zeros_like(left)), tz_ref[...])
        for h in range(chunks):
            spec_ref[h * per_row + c] = done[h * half_y : (h + 1) * half_y]

    def block(g, carry):
        at = [pl.ds(pl.multiple_of(g * 16 + 8 * k, 8), 8) for k in range(2)]
        pooled = jnp.concatenate([pooled_ref[:, a, :].reshape(channels * 8, 128) for a in at], 1)
        spectral = jnp.concatenate([spec_ref[:, a, :].reshape(channels * 8, 128) for a in at], 1)
        level = gelu(dot_left3(lift_ref[...], pooled) + spectral)
        added = dot_left3(proj_ref[...], level)
        for k in range(2):
            for b in range(2):
                piece = added[b * channels * 8 : (b + 1) * channels * 8, k * 128 : (k + 1) * 128]
                piece = piece.reshape(channels, 8, 128)
                rows = pl.ds(pl.multiple_of(g * 32 + 16 * k + 8 * b, 8), 8)
                for x in range(local_x):
                    out_ref[:, x, rows, :] = base_ref[:, x, rows, :] + piece
        return carry

    lax.fori_loop(0, half_y // 16, block, 0)


def exchange(values, axis_size):
    rows = values.shape[0] // axis_size
    flat = values.reshape(axis_size, rows, 128)
    return lax.all_to_all(flat, "gx", split_axis=0, concat_axis=0, tiled=True)


def on_device(features, fine_weights, middle_weights, lift_fine, lift_middle, project_out):
    channels, local_x, cells_y, cells_z = features.shape
    n = lax.axis_size("gx")
    owned = fine_weights.shape[0]
    owned_c = middle_weights.shape[0]
    half_ky, half_kz = KY // 2, KZ // 2
    narrow = 8
    fits = (
        owned % KZ == 0
        and owned_c % narrow == 0
        and local_x == 2
        and cells_z == 128
        and cells_y % 32 == 0
        and channels % 16 == 0
    )
    if not fits:
        return general_device(
            features, fine_weights, middle_weights, lift_fine, lift_middle, project_out
        )
    modes_x = fine_weights.shape[1]
    modes_c = middle_weights.shape[1]
    per_row = 128 // KZ
    chunks = channels // per_row
    tx = jnp.asarray(host_table(modes_x, local_x * n), F32).reshape(modes_x, n, local_x)
    txc = jnp.asarray(host_table(modes_c, n), F32)
    lift = blockwise(lift_fine, np.eye(8))
    proj = blockwise(project_out, np.eye(8))
    liftm = blockwise(lift_middle, np.eye(8))
    spread = np.repeat(np.eye(8), 2, axis=0)
    projm = jnp.concatenate(
        [blockwise(project_out, spread[8 * b : 8 * b + 8]) for b in range(2)], 0
    )

    coeffs = forward_fine(features, KY, KZ)
    got = exchange(coeffs, n)
    got = got.reshape(n, owned // KZ, local_x, channels, KZ)
    modal = jnp.einsum("aixcj,kax->ijkc", got, tx, precision=HIGHEST)
    modal = modal.reshape(owned, modes_x, channels)
    mixed = mix_modes(modal, fine_weights).reshape(owned // KZ, KZ, modes_x, channels)
    back = jnp.einsum("ijko,kax->aixoj", mixed, tx, precision=HIGHEST)
    slab = exchange(back.reshape(-1, 128), n).reshape(-1, 128)

    half_y, half_z = cells_y // 2, cells_z // 2
    pool_y = np.repeat(np.eye(half_y), 2, axis=1) * 0.5
    pool_z = np.repeat(np.eye(half_z), 2, axis=1) * 0.25
    ty_c = host_table(half_ky, half_y)
    tz_c = host_table(half_kz, half_z)
    parts = half_kz // narrow
    per_c = 128 // narrow
    chunks_c = channels // per_c
    yc = left_rows(np.concatenate([pool_y, ty_c @ pool_y], 0))
    zc_full = (tz_c @ pool_z).T.reshape(cells_z, parts, 1, narrow)
    zc = right_three(np.broadcast_to(zc_full, (cells_z, parts, per_c, narrow)).reshape(cells_z, -1))
    zp = np.repeat(pool_z, 2, axis=0).T
    zp = np.asarray(zp, jnp.bfloat16)
    zp = jnp.asarray(np.concatenate([zp, zp], 0))
    ty_i = left_three(host_table(KY, cells_y).T)
    tz_i = right_three(np.tile(host_table(KZ, cells_z), (per_row, 1)))
    base, pooled, coarse = pl.pallas_call(
        middle_kernel,
        out_shape=(
            jax.ShapeDtypeStruct(features.shape, F32),
            jax.ShapeDtypeStruct((channels, half_y, 128), F32),
            jax.ShapeDtypeStruct((half_ky * parts * chunks_c, 128), F32),
        ),
        in_specs=[whole()] * 9,
        out_specs=(whole(), whole(), whole()),
        scratch_shapes=[
            pltpu.VMEM(features.shape, F32),
            pltpu.VMEM((channels, cells_y, cells_z), F32),
        ],
        name="middle",
    )(slab, features, ty_i, tz_i, lift, proj, yc, zc, zp)

    got = exchange(coarse, n).reshape(n, owned_c // narrow, chunks_c, per_c, narrow)
    modal = jnp.einsum("aqhlj,ka->qjkhl", got, txc, precision=HIGHEST)
    mixed = mix_modes(modal.reshape(owned_c, modes_c, channels), middle_weights)
    mixed = mixed.reshape(owned_c // narrow, narrow, modes_c, chunks_c, per_c)
    back = jnp.einsum("qjkhl,ka->aqhlj", mixed, txc, precision=HIGHEST)
    slab = exchange(back.reshape(-1, 128), n).reshape(-1, 128)

    tyc_i = left_three(ty_c.T)
    grown = np.repeat(tz_c, 2, axis=1).reshape(parts, 1, narrow, cells_z)
    tzc_i = right_three(np.broadcast_to(grown, (parts, per_c, narrow, cells_z)).reshape(-1, cells_z))
    return pl.pallas_call(
        final_kernel,
        out_shape=jax.ShapeDtypeStruct(features.shape, F32),
        in_specs=[whole()] * 7,
        out_specs=whole(),
        scratch_shapes=[pltpu.VMEM((channels, half_y, 128), F32)],
        name="final",
    )(slab, pooled, base, tyc_i, tzc_i, liftm, projm)


def solution(mesh):
    in_specs = (
        P(None, ("groups", "gx"), None, None),
        P("gx", None, None, None),
        P("gx", None, None, None),
        P(),
        P(),
        P(),
    )
    out_specs = P(None, ("groups", "gx"), None, None)
    return jax.shard_map(
        on_device, mesh=mesh, in_specs=in_specs, out_specs=out_specs, check_vma=False
    )
```

```python
import functools

import jax
import jax.numpy as jnp
import numpy as np
from jax import lax
from jax.experimental import pallas as pl
from jax.experimental.pallas import tpu as pltpu
from jax.sharding import PartitionSpec as P

KY = 48
KZ = 32


HIGHEST = lax.Precision.HIGHEST


def cosine_table(modes_kept, length, columns):
    orders = jnp.arange(modes_kept, dtype=jnp.int32)[:, None]
    points = jnp.arange(columns, dtype=jnp.int32)[None, :]
    phase = orders * (2 * points + 1) % (4 * length)
    angle = jnp.pi / (2 * length) * phase.astype(jnp.float32)
    scales = jnp.where(
        orders == 0, jnp.sqrt(jnp.float32(1.0 / length)), jnp.sqrt(jnp.float32(2.0 / length))
    )
    return scales * jnp.cos(angle)


def forward_yz(values, modes_y, modes_z):
    channels, local_x, cells_y, cells_z = values.shape
    table_z = cosine_table(modes_z, cells_z, cells_z)
    table_y = cosine_table(modes_y, cells_y, cells_y)
    along_z = jnp.einsum("cxyz,jz->cxyj", values, table_z, precision=HIGHEST)
    both = jnp.einsum("cxyj,iy->ijxc", along_z, table_y, precision=HIGHEST)
    return both.reshape(modes_y * modes_z, local_x, channels)


def inverse_yz(coeffs, modes_y, modes_z, cells_y, cells_z):
    total, local_x, channels = coeffs.shape
    shaped = coeffs.reshape(modes_y, modes_z, local_x, channels)
    table_z = cosine_table(modes_z, cells_z, cells_z)
    table_y = cosine_table(modes_y, cells_y, cells_y)
    along_y = jnp.einsum("ijxc,iy->jxcy", shaped, table_y, precision=HIGHEST)
    return jnp.einsum("jxcy,jz->cxyz", along_y, table_z, precision=HIGHEST)


def mix_modes(modal, weights):
    return jnp.einsum(
        "mkc,mkco->mko", modal.astype(jnp.bfloat16), weights, preferred_element_type=jnp.float32
    )


def pointwise(values, matrix):
    return jnp.einsum("cxyz,co->oxyz", values, matrix, precision=HIGHEST)


def coarsen(values):
    channels, cells_x, cells_y, cells_z = values.shape
    shaped = values.reshape(channels, cells_x // 2, 2, cells_y // 2, 2, cells_z // 2, 2)
    return jnp.mean(shaped, axis=(2, 4, 6))


def refine(values):
    return jnp.repeat(jnp.repeat(jnp.repeat(values, 2, axis=1), 2, axis=2), 2, axis=3)


def general_device(features, fine_weights, middle_weights, lift_fine, lift_middle, project_out):
    channels, local_x, cells_y, cells_z = features.shape
    group_size = lax.axis_size("gx")
    cells_x = local_x * group_size
    modes_x = fine_weights.shape[1]
    coeffs = forward_yz(features, KY, KZ)
    table_x = cosine_table(modes_x, cells_x, cells_x)
    owned_pairs = coeffs.shape[0] // group_size
    grouped = coeffs.reshape(group_size, owned_pairs, local_x, channels)
    modal = jnp.einsum(
        "amxc,kx->mkc",
        lax.all_to_all(grouped, "gx", split_axis=0, concat_axis=2, tiled=True),
        table_x,
        precision=HIGHEST,
    )
    mixed = mix_modes(modal, fine_weights)
    back = jnp.einsum("mkc,kx->mxc", mixed, table_x, precision=HIGHEST)
    slabs = lax.all_to_all(back, "gx", split_axis=1, concat_axis=0, tiled=True)
    level_one = jax.nn.gelu(
        inverse_yz(slabs, KY, KZ, cells_y, cells_z) + pointwise(features, lift_fine),
        approximate=False,
    )
    pooled = coarsen(level_one)
    half_x = local_x // 2
    half_ky = KY // 2
    half_kz = KZ // 2
    half_modes = middle_weights.shape[1]
    coarse_x = half_x * group_size
    coarse_coeffs = forward_yz(pooled, half_ky, half_kz)
    coarse_pencils = lax.all_to_all(coarse_coeffs, "gx", split_axis=0, concat_axis=1, tiled=True)
    coarse_table = cosine_table(half_modes, coarse_x, coarse_x)
    coarse_modal = jnp.einsum("mxc,kx->mkc", coarse_pencils, coarse_table, precision=HIGHEST)
    coarse_mixed = mix_modes(coarse_modal, middle_weights)
    coarse_back = jnp.einsum("mkc,kx->mxc", coarse_mixed, coarse_table, precision=HIGHEST)
    coarse_slabs = lax.all_to_all(coarse_back, "gx", split_axis=1, concat_axis=0, tiled=True)
    level_two = jax.nn.gelu(
        inverse_yz(coarse_slabs, half_ky, half_kz, cells_y // 2, cells_z // 2)
        + pointwise(pooled, lift_middle),
        approximate=False,
    )
    return features + pointwise(level_one + refine(level_two), project_out)


BF16 = jnp.bfloat16
MESH = pl.DeviceIdType.MESH
F32 = jnp.float32


def host_table(modes_kept, length):
    orders = np.arange(modes_kept)[:, None]
    points = np.arange(length)[None, :]
    scales = np.where(orders == 0, np.sqrt(1.0 / length), np.sqrt(2.0 / length))
    return scales * np.cos(np.pi * orders * (2 * points + 1) / (2 * length))


def host_split(table):
    table = np.asarray(table, np.float32)
    high = table.astype(jnp.bfloat16)
    low = (table - high.astype(np.float32)).astype(jnp.bfloat16)
    return high, low


def left_rows(table):
    high, low = host_split(table)
    return jnp.asarray(
        np.concatenate([np.concatenate([high, high], 1), np.concatenate([low, low], 1)], 0)
    )


def left_three(table):
    high, low = host_split(table)
    return jnp.asarray(np.concatenate([high, high, low], 1))


def right_three(table):
    high, low = host_split(table)
    return jnp.asarray(np.concatenate([high, high, low], 0))


def split(values):
    high = values.astype(BF16)
    low = (values - high.astype(F32)).astype(BF16)
    return high, low


def dot(left, right):
    return jnp.dot(left, right, preferred_element_type=F32)


def dot_left3(left3, values):
    high, low = split(values)
    return dot(left3, jnp.concatenate([high, low, high], 0))


def dot_right3(values, right3):
    high, low = split(values)
    return dot(jnp.concatenate([high, low, high], 1), right3)


def gelu(t):
    return 0.5 * t * (1.0 + lax.erf(t * np.float32(np.sqrt(0.5))))


def whole():
    return pl.BlockSpec(memory_space=pltpu.VMEM)


def forward_kernel(f_ref, ty_ref, tz_ref, out_ref, grown_ref):
    step = pl.program_id(0)
    block, local_x, cells_y, cells_z = f_ref.shape
    modes = ty_ref.shape[0] // 2
    n = out_ref.shape[0]
    per = modes // n
    rows = grown_ref.shape[0] // modes
    channels = rows // local_x
    half = channels // 2
    for c in range(block):
        wide = jnp.concatenate([f_ref[c, x] for x in range(local_x)], 1)
        high, low = split(wide)
        both = dot(ty_ref[...], jnp.concatenate([high, low], 0))
        both = both[:modes] + both[modes:]
        for x in range(local_x):
            grown_ref[pl.ds(x * channels + step * block + c, modes, stride=rows), :] = both[
                :, x * cells_z : (x + 1) * cells_z
            ]

    @pl.when(step == pl.num_programs(0) - 1)
    def _():
        lane = lax.broadcasted_iota(jnp.int32, (3 * half, 128), 1) // 32

        def owner(a, carry):
            at = pl.multiple_of(a * per * rows, 8)
            done = dot_right3(grown_ref[pl.ds(at, per * rows), :], tz_ref[...])
            total = jnp.concatenate([done[g * rows + 3 * half : (g + 1) * rows] for g in range(per)], 0)
            for g in range(per):
                total = jnp.where(lane == g, done[g * rows : g * rows + 3 * half], total)
            out_ref[a] = total
            return carry

        lax.fori_loop(0, n, owner, 0)


def forward_fine(features, modes_y, modes_z, n):
    channels, local_x, cells_y, cells_z = features.shape
    block = 4
    ty = left_rows(host_table(modes_y, cells_y))
    tz = right_three(np.tile(host_table(modes_z, cells_z).T, (1, 4)))
    shape = (n, modes_y // n * channels // 2, 128)
    return pl.pallas_call(
        forward_kernel,
        grid=(channels // block,),
        out_shape=jax.ShapeDtypeStruct(shape, F32),
        in_specs=[
            pl.BlockSpec((block, local_x, cells_y, cells_z), lambda h: (h, 0, 0, 0)),
            pl.BlockSpec(ty.shape, lambda h: (0, 0)),
            pl.BlockSpec(tz.shape, lambda h: (0, 0)),
        ],
        out_specs=pl.BlockSpec(shape, lambda h: (0, 0, 0)),
        scratch_shapes=[pltpu.VMEM((modes_y * local_x * channels, cells_z), F32)],
        name="forward_fine",
    )(features, ty, tz)


def middle_kernel(
    slab_ref, f_ref, ty_ref, tz_ref, lift_ref, proj_ref, yc_ref, zc_ref, zp_ref,
    base_ref, pooled_ref, coarse_ref, spec_ref, sum_ref, grown_ref,
):
    channels, local_x, cells_y, cells_z = f_ref.shape
    modes_y = ty_ref.shape[1] // 3
    n = slab_ref.shape[0]
    per = modes_y // n
    half = channels // 2
    rows = 2 * channels
    lane = lax.broadcasted_iota(jnp.int32, (rows, 128), 1) // 32
    tail = lax.broadcasted_iota(jnp.int32, (rows, 128), 0) >= 3 * half

    def inverse(a, carry):
        lefts = []
        for g in range(per):
            value = jnp.concatenate([slab_ref[a], slab_ref[a, g * half : (g + 1) * half]], 0)
            lefts.append(jnp.where(lane == jnp.where(tail, 3, g), value, 0.0))
        done = dot_right3(jnp.concatenate(lefts, 0), tz_ref[...])
        grown_ref[pl.ds(pl.multiple_of(a * per * rows, 8), per * rows), :] = done
        return carry

    lax.fori_loop(0, n, inverse, 0)

    def inverse_y(o, carry):
        wide = jnp.concatenate(
            [grown_ref[pl.ds(x * channels + o, modes_y, stride=rows), :] for x in range(local_x)], 1
        )
        done = dot_left3(ty_ref[...], wide)
        for x in range(local_x):
            spec_ref[o, x] = done[:, x * cells_z : (x + 1) * cells_z]
        return carry

    lax.fori_loop(0, channels, inverse_y, 0, unroll=4)

    def block(b, carry):
        at = pl.ds(pl.multiple_of(b * 8, 8), 8)
        values = jnp.concatenate(
            [f_ref[:, x, at, :].reshape(channels * 8, cells_z) for x in range(local_x)], 1
        )
        spectral = jnp.concatenate(
            [spec_ref[:, x, at, :].reshape(channels * 8, cells_z) for x in range(local_x)], 1
        )
        level = gelu(dot_left3(lift_ref[...], values) + spectral)
        base = values + dot_left3(proj_ref[...], level)
        for x in range(local_x):
            base_ref[:, x, at, :] = base[:, x * cells_z : (x + 1) * cells_z].reshape(channels, 8, cells_z)
        sum_ref[:, at, :] = (level[:, :cells_z] + level[:, cells_z:]).reshape(channels, 8, cells_z)
        return carry

    lax.fori_loop(0, cells_y // 8, block, 0)

    half_y = cells_y // 2
    modes_c = yc_ref.shape[0] // 2 - half_y
    parts = zc_ref.shape[1] // 128
    coarse_chunks = coarse_ref.shape[0] // (modes_c * parts)
    coarse_per = channels // coarse_chunks
    coarse_lane = (
        lax.broadcasted_iota(jnp.int32, (modes_c, parts * 128), 1) // (128 // coarse_per) % coarse_per
    )
    rows = modes_c + half_y

    def coarse(h, carry):
        total = jnp.zeros((modes_c, parts * 128), F32)
        for pair in range(coarse_per // 2):
            first = h * coarse_per + pair * 2
            wide = jnp.concatenate([sum_ref[first], sum_ref[first + 1]], 1)
            high, low = split(wide)
            both = dot(yc_ref[...], jnp.concatenate([high, low], 0))
            both = both[:rows] + both[rows:]
            modal = jnp.concatenate([both[half_y:, :128], both[half_y:, 128:]], 0)
            done = dot_right3(modal, zc_ref[...])
            for k in range(2):
                total = jnp.where(
                    coarse_lane == pair * 2 + k, done[k * modes_c : (k + 1) * modes_c], total
                )
            flat = jnp.concatenate([both[:half_y, :128], both[:half_y, 128:]], 0)
            high, low = split(flat)
            mean = dot(jnp.concatenate([high, low], 1), zp_ref[...])
            pooled_ref[first] = mean[:half_y]
            pooled_ref[first + 1] = mean[half_y:]
        for p in range(parts):
            coarse_ref[pl.ds(p * coarse_chunks + h, modes_c, stride=parts * coarse_chunks), :] = total[
                :, p * 128 : (p + 1) * 128
            ]
        return carry

    lax.fori_loop(0, coarse_chunks, coarse, 0)


def prepare_kernel(lift_ref, middle_ref, out_ref, lift_wide, middle_wide, proj_wide, final_wide):
    channels = lift_ref.shape[0]
    size = channels * 8
    row = lax.broadcasted_iota(jnp.int32, (size, channels), 0) // 8
    pick = (row == lax.broadcasted_iota(jnp.int32, (size, channels), 1)).astype(F32).astype(BF16)
    col = lax.broadcasted_iota(jnp.int32, (channels, size), 1) // 8
    place = (col == lax.broadcasted_iota(jnp.int32, (channels, size), 0)).astype(F32).astype(BF16)
    left = lax.broadcasted_iota(jnp.int32, (size, size), 0) % 8
    right = lax.broadcasted_iota(jnp.int32, (size, size), 1) % 8

    def fill(matrix_ref, targets):
        for part, spots in zip(split(matrix_ref[...]), ((0, 1), (2,))):
            grown = lax.dot_general(pick, part, (((1,), (1,)), ((), ())), preferred_element_type=F32)
            grown = dot(grown.astype(BF16), place)
            for ref, at, rule in targets:
                value = jnp.where(rule, grown, 0.0).astype(BF16)
                for spot in spots:
                    ref[at : at + size, spot * size : (spot + 1) * size] = value

    same = left == right
    fill(lift_ref, ((lift_wide, 0, same),))
    fill(middle_ref, ((middle_wide, 0, same),))
    fill(
        out_ref,
        ((proj_wide, 0, same), (final_wide, 0, left // 2 == right), (final_wide, size, left // 2 + 4 == right)),
    )


def prepare(lift_fine, lift_middle, project_out):
    size = lift_fine.shape[0] * 8
    shape = jax.ShapeDtypeStruct((size, 3 * size), BF16)
    return pl.pallas_call(
        prepare_kernel,
        out_shape=(shape, shape, shape, jax.ShapeDtypeStruct((2 * size, 3 * size), BF16)),
        in_specs=[whole()] * 3,
        out_specs=(whole(),) * 4,
        name="prepare",
    )(lift_fine, lift_middle, project_out)


def greet(n):
    me = lax.axis_index("gx")
    barrier = pltpu.get_barrier_semaphore()
    for d in range(1, n):
        pl.semaphore_signal(barrier, 1, device_id={"gx": lax.rem(me + d, n)}, device_id_type=MESH)
    pl.semaphore_wait(barrier, n - 1)


def swap(n, source, target, send_sem, recv_sem, own_sem):
    me = lax.axis_index("gx")
    copies = []
    for d in range(1, n):
        peer = lax.rem(me + d, n)
        copy = pltpu.make_async_remote_copy(
            src_ref=source.at[peer],
            dst_ref=target.at[me],
            send_sem=send_sem.at[d],
            recv_sem=recv_sem.at[d],
            device_id={"gx": peer},
            device_id_type=MESH,
        )
        copy.start()
        copies.append(copy)
    own = pltpu.make_async_copy(source.at[me], target.at[me], own_sem)
    own.start()
    for copy in copies:
        copy.wait()
    own.wait()


def exchange_kernel(n, in_ref, out_ref, send_sem, recv_sem, own_sem):
    greet(n)
    swap(n, in_ref, out_ref, send_sem, recv_sem, own_sem)


def exchange(values, n, number):
    return pl.pallas_call(
        functools.partial(exchange_kernel, n),
        out_shape=jax.ShapeDtypeStruct(values.shape, F32),
        in_specs=[whole()],
        out_specs=whole(),
        scratch_shapes=[
            pltpu.SemaphoreType.DMA((n,)),
            pltpu.SemaphoreType.DMA((n,)),
            pltpu.SemaphoreType.DMA,
        ],
        compiler_params=pltpu.CompilerParams(collective_id=number, has_side_effects=True),
        name="exchange",
    )(values)


def mix_kernel(
    n, tx, wire_ref, w_hbm, out_ref, got, w_ref, modal, mixed, back,
    send_one, recv_one, send_two, recv_two, own_sem, w_sem,
):
    modes_x, channels, _, owned = w_ref.shape
    half = channels // 2
    fetch = pltpu.make_async_copy(w_hbm, w_ref, w_sem)
    fetch.start()
    greet(n)
    swap(n, wire_ref, got, send_one, recv_one, own_sem.at[0])
    fetch.wait()
    lane = lax.broadcasted_iota(jnp.int32, (half, 128), 1)
    for k in range(modes_x):
        first = sum(got[a, :channels] * np.float32(tx[k, a, 0]) for a in range(n))
        second = sum(got[a] * np.float32(tx[k, a, 1]) for a in range(n))
        extra = jnp.zeros((half, 128), F32)
        for g in range(3):
            piece = pltpu.roll(second[g * half : (g + 1) * half], 32 * (g + 1), 1)
            extra = jnp.where(lane // 32 == g, piece, extra)
        total = first + jnp.concatenate([second[channels:], extra], 0)
        modal[k] = total.astype(BF16).astype(F32)
    mixed[...] = jnp.zeros_like(mixed)

    def mode(k, carry):
        total = jnp.zeros((channels, owned), F32)
        for c in range(channels):
            total += modal[k, c : c + 1, :owned] * w_ref[k, c].astype(F32)
        mixed[k, :, :owned] = total
        return carry

    lax.fori_loop(0, modes_x, mode, 0)
    wide = lax.broadcasted_iota(jnp.int32, (3 * half, 128), 1)
    for a in range(n):
        first = sum(mixed[k] * np.float32(tx[k, a, 0]) for k in range(modes_x))
        second = sum(mixed[k] * np.float32(tx[k, a, 1]) for k in range(modes_x))
        rolled = jnp.concatenate([pltpu.roll(second[half:], 96 - 32 * g, 1) for g in range(3)], 0)
        back[a] = jnp.where(wide < 96, jnp.concatenate([first, second[:half]], 0), rolled)
    swap(n, back, out_ref, send_two, recv_two, own_sem.at[1])


def mix_fine(wire, weights, tx, n):
    turned = jnp.transpose(weights, (1, 2, 3, 0))
    modes_x, channels = turned.shape[:2]
    return pl.pallas_call(
        functools.partial(mix_kernel, n, tx),
        out_shape=jax.ShapeDtypeStruct(wire.shape, F32),
        in_specs=[whole(), pl.BlockSpec(memory_space=pl.ANY)],
        out_specs=whole(),
        scratch_shapes=[
            pltpu.VMEM(wire.shape, F32),
            pltpu.VMEM(turned.shape, BF16),
            pltpu.VMEM((modes_x, channels, 128), F32),
            pltpu.VMEM((modes_x, channels, 128), F32),
            pltpu.VMEM(wire.shape, F32),
        ]
        + [pltpu.SemaphoreType.DMA((n,))] * 4
        + [pltpu.SemaphoreType.DMA((2,)), pltpu.SemaphoreType.DMA],
        compiler_params=pltpu.CompilerParams(collective_id=0, has_side_effects=True),
        name="mix_fine",
    )(wire, turned)


def final_kernel(
    slab_ref, pooled_ref, base_ref, ty_ref, tz_ref, lift_ref, proj_ref, out_ref, spec_ref
):
    channels, half_y, _ = pooled_ref.shape
    local_x = base_ref.shape[1]
    modes = ty_ref.shape[1] // 3
    rows_per_mode = slab_ref.shape[0] // modes
    parts = tz_ref.shape[0] // (3 * 128)
    chunks = rows_per_mode // parts
    per_row = channels // chunks
    stacked = []
    for h in range(chunks):
        wide = jnp.concatenate(
            [slab_ref[pl.ds(p * chunks + h, modes, stride=rows_per_mode), :] for p in range(parts)], 1
        )
        stacked.append(dot_left3(ty_ref[...], wide))
    grown = jnp.concatenate(stacked, 0)
    high, low = split(grown)
    left = jnp.concatenate([high, low, high], 1)
    lane = lax.broadcasted_iota(jnp.int32, left.shape, 1) // (128 // per_row) % per_row

    for c in range(per_row):
        done = dot(jnp.where(lane == c, left, jnp.zeros_like(left)), tz_ref[...])
        for h in range(chunks):
            spec_ref[h * per_row + c] = done[h * half_y : (h + 1) * half_y]

    def block(g, carry):
        at = [pl.ds(pl.multiple_of(g * 16 + 8 * k, 8), 8) for k in range(2)]
        pooled = jnp.concatenate([pooled_ref[:, a, :].reshape(channels * 8, 128) for a in at], 1)
        spectral = jnp.concatenate([spec_ref[:, a, :].reshape(channels * 8, 128) for a in at], 1)
        level = gelu(dot_left3(lift_ref[...], pooled) + spectral)
        added = dot_left3(proj_ref[...], level)
        for k in range(2):
            for b in range(2):
                piece = added[b * channels * 8 : (b + 1) * channels * 8, k * 128 : (k + 1) * 128]
                piece = piece.reshape(channels, 8, 128)
                rows = pl.ds(pl.multiple_of(g * 32 + 16 * k + 8 * b, 8), 8)
                for x in range(local_x):
                    out_ref[:, x, rows, :] = base_ref[:, x, rows, :] + piece
        return carry

    lax.fori_loop(0, half_y // 16, block, 0)


def on_device(features, fine_weights, middle_weights, lift_fine, lift_middle, project_out):
    channels, local_x, cells_y, cells_z = features.shape
    n = lax.axis_size("gx")
    owned = fine_weights.shape[0]
    owned_c = middle_weights.shape[0]
    half_ky, half_kz = KY // 2, KZ // 2
    narrow = 8
    fits = (
        owned == 3 * KZ
        and KZ == 32
        and KY == 3 * n
        and owned_c % narrow == 0
        and local_x == 2
        and cells_z == 128
        and cells_y % 32 == 0
        and channels % 16 == 0
    )
    if not fits:
        return general_device(
            features, fine_weights, middle_weights, lift_fine, lift_middle, project_out
        )
    modes_x = fine_weights.shape[1]
    modes_c = middle_weights.shape[1]
    tx = np.asarray(host_table(modes_x, local_x * n), np.float32).reshape(modes_x, n, local_x)
    txc = jnp.asarray(host_table(modes_c, n), F32)
    lift, liftm, proj, projm = prepare(lift_fine, lift_middle, project_out)
    wire = forward_fine(features, KY, KZ, n)
    slab = mix_fine(wire, fine_weights, tx, n)

    half_y, half_z = cells_y // 2, cells_z // 2
    pool_y = np.repeat(np.eye(half_y), 2, axis=1) * 0.5
    pool_z = np.repeat(np.eye(half_z), 2, axis=1) * 0.25
    ty_c = host_table(half_ky, half_y)
    tz_c = host_table(half_kz, half_z)
    parts = half_kz // narrow
    per_c = 128 // narrow
    chunks_c = channels // per_c
    yc = left_rows(np.concatenate([pool_y, ty_c @ pool_y], 0))
    zc_full = (tz_c @ pool_z).T.reshape(cells_z, parts, 1, narrow)
    zc = right_three(np.broadcast_to(zc_full, (cells_z, parts, per_c, narrow)).reshape(cells_z, -1))
    zp = np.repeat(pool_z, 2, axis=0).T
    zp = np.asarray(zp, jnp.bfloat16)
    zp = jnp.asarray(np.concatenate([zp, zp], 0))
    ty_i = left_three(host_table(KY, cells_y).T)
    tz_i = right_three(np.tile(host_table(KZ, cells_z), (4, 1)))
    base, pooled, coarse = pl.pallas_call(
        middle_kernel,
        out_shape=(
            jax.ShapeDtypeStruct(features.shape, F32),
            jax.ShapeDtypeStruct((channels, half_y, 128), F32),
            jax.ShapeDtypeStruct((half_ky * parts * chunks_c, 128), F32),
        ),
        in_specs=[whole()] * 9,
        out_specs=(whole(), whole(), whole()),
        scratch_shapes=[
            pltpu.VMEM(features.shape, F32),
            pltpu.VMEM((channels, cells_y, cells_z), F32),
            pltpu.VMEM((KY * local_x * channels, cells_z), F32),
        ],
        name="middle",
    )(slab, features, ty_i, tz_i, lift, proj, yc, zc, zp)

    count = owned_c // narrow
    got = exchange(coarse.reshape(n, -1, 128), n, 1).reshape(n, -1)
    modal = jnp.einsum("ar,ka->kr", got, txc, precision=HIGHEST)
    modal = modal.reshape(modes_c, count, channels, narrow).transpose(1, 3, 0, 2)
    mixed = mix_modes(modal.reshape(owned_c, modes_c, channels), middle_weights)
    mixed = mixed.reshape(count, narrow, modes_c, channels).transpose(2, 0, 3, 1)
    back = jnp.einsum("kr,ka->ar", mixed.reshape(modes_c, -1), txc, precision=HIGHEST)
    slab = exchange(back.reshape(n, -1, 128), n, 2).reshape(-1, 128)

    tyc_i = left_three(ty_c.T)
    grown = np.repeat(tz_c, 2, axis=1).reshape(parts, 1, narrow, cells_z)
    tzc_i = right_three(np.broadcast_to(grown, (parts, per_c, narrow, cells_z)).reshape(-1, cells_z))
    return pl.pallas_call(
        final_kernel,
        out_shape=jax.ShapeDtypeStruct(features.shape, F32),
        in_specs=[whole()] * 7,
        out_specs=whole(),
        scratch_shapes=[pltpu.VMEM((channels, half_y, 128), F32)],
        name="final",
    )(slab, pooled, base, tyc_i, tzc_i, liftm, projm)


def solution(mesh):
    in_specs = (
        P(None, ("groups", "gx"), None, None),
        P("gx", None, None, None),
        P("gx", None, None, None),
        P(),
        P(),
        P(),
    )
    out_specs = P(None, ("groups", "gx"), None, None)
    return jax.shard_map(
        on_device, mesh=mesh, in_specs=in_specs, out_specs=out_specs, check_vma=False
    )
```

```python
import functools

import jax
import jax.numpy as jnp
import numpy as np
from jax import lax
from jax.experimental import pallas as pl
from jax.experimental.pallas import tpu as pltpu
from jax.sharding import PartitionSpec as P

KY = 48
KZ = 32


HIGHEST = lax.Precision.HIGHEST


def cosine_table(modes_kept, length, columns):
    orders = jnp.arange(modes_kept, dtype=jnp.int32)[:, None]
    points = jnp.arange(columns, dtype=jnp.int32)[None, :]
    phase = orders * (2 * points + 1) % (4 * length)
    angle = jnp.pi / (2 * length) * phase.astype(jnp.float32)
    scales = jnp.where(
        orders == 0, jnp.sqrt(jnp.float32(1.0 / length)), jnp.sqrt(jnp.float32(2.0 / length))
    )
    return scales * jnp.cos(angle)


def forward_yz(values, modes_y, modes_z):
    channels, local_x, cells_y, cells_z = values.shape
    table_z = cosine_table(modes_z, cells_z, cells_z)
    table_y = cosine_table(modes_y, cells_y, cells_y)
    along_z = jnp.einsum("cxyz,jz->cxyj", values, table_z, precision=HIGHEST)
    both = jnp.einsum("cxyj,iy->ijxc", along_z, table_y, precision=HIGHEST)
    return both.reshape(modes_y * modes_z, local_x, channels)


def inverse_yz(coeffs, modes_y, modes_z, cells_y, cells_z):
    total, local_x, channels = coeffs.shape
    shaped = coeffs.reshape(modes_y, modes_z, local_x, channels)
    table_z = cosine_table(modes_z, cells_z, cells_z)
    table_y = cosine_table(modes_y, cells_y, cells_y)
    along_y = jnp.einsum("ijxc,iy->jxcy", shaped, table_y, precision=HIGHEST)
    return jnp.einsum("jxcy,jz->cxyz", along_y, table_z, precision=HIGHEST)


def mix_modes(modal, weights):
    return jnp.einsum(
        "mkc,mkco->mko", modal.astype(jnp.bfloat16), weights, preferred_element_type=jnp.float32
    )


def pointwise(values, matrix):
    return jnp.einsum("cxyz,co->oxyz", values, matrix, precision=HIGHEST)


def coarsen(values):
    channels, cells_x, cells_y, cells_z = values.shape
    shaped = values.reshape(channels, cells_x // 2, 2, cells_y // 2, 2, cells_z // 2, 2)
    return jnp.mean(shaped, axis=(2, 4, 6))


def refine(values):
    return jnp.repeat(jnp.repeat(jnp.repeat(values, 2, axis=1), 2, axis=2), 2, axis=3)


def general_device(features, fine_weights, middle_weights, lift_fine, lift_middle, project_out):
    channels, local_x, cells_y, cells_z = features.shape
    group_size = lax.axis_size("gx")
    cells_x = local_x * group_size
    modes_x = fine_weights.shape[1]
    coeffs = forward_yz(features, KY, KZ)
    table_x = cosine_table(modes_x, cells_x, cells_x)
    owned_pairs = coeffs.shape[0] // group_size
    grouped = coeffs.reshape(group_size, owned_pairs, local_x, channels)
    modal = jnp.einsum(
        "amxc,kx->mkc",
        lax.all_to_all(grouped, "gx", split_axis=0, concat_axis=2, tiled=True),
        table_x,
        precision=HIGHEST,
    )
    mixed = mix_modes(modal, fine_weights)
    back = jnp.einsum("mkc,kx->mxc", mixed, table_x, precision=HIGHEST)
    slabs = lax.all_to_all(back, "gx", split_axis=1, concat_axis=0, tiled=True)
    level_one = jax.nn.gelu(
        inverse_yz(slabs, KY, KZ, cells_y, cells_z) + pointwise(features, lift_fine),
        approximate=False,
    )
    pooled = coarsen(level_one)
    half_x = local_x // 2
    half_ky = KY // 2
    half_kz = KZ // 2
    half_modes = middle_weights.shape[1]
    coarse_x = half_x * group_size
    coarse_coeffs = forward_yz(pooled, half_ky, half_kz)
    coarse_pencils = lax.all_to_all(coarse_coeffs, "gx", split_axis=0, concat_axis=1, tiled=True)
    coarse_table = cosine_table(half_modes, coarse_x, coarse_x)
    coarse_modal = jnp.einsum("mxc,kx->mkc", coarse_pencils, coarse_table, precision=HIGHEST)
    coarse_mixed = mix_modes(coarse_modal, middle_weights)
    coarse_back = jnp.einsum("mkc,kx->mxc", coarse_mixed, coarse_table, precision=HIGHEST)
    coarse_slabs = lax.all_to_all(coarse_back, "gx", split_axis=1, concat_axis=0, tiled=True)
    level_two = jax.nn.gelu(
        inverse_yz(coarse_slabs, half_ky, half_kz, cells_y // 2, cells_z // 2)
        + pointwise(pooled, lift_middle),
        approximate=False,
    )
    return features + pointwise(level_one + refine(level_two), project_out)


BF16 = jnp.bfloat16
MESH = pl.DeviceIdType.MESH
F32 = jnp.float32


def host_table(modes_kept, length):
    orders = np.arange(modes_kept)[:, None]
    points = np.arange(length)[None, :]
    scales = np.where(orders == 0, np.sqrt(1.0 / length), np.sqrt(2.0 / length))
    return scales * np.cos(np.pi * orders * (2 * points + 1) / (2 * length))


def host_split(table):
    table = np.asarray(table, np.float32)
    high = table.astype(jnp.bfloat16)
    low = (table - high.astype(np.float32)).astype(jnp.bfloat16)
    return high, low


def left_rows(table):
    high, low = host_split(table)
    return jnp.asarray(
        np.concatenate([np.concatenate([high, high], 1), np.concatenate([low, low], 1)], 0)
    )


def left_three(table):
    high, low = host_split(table)
    return jnp.asarray(np.concatenate([high, high, low], 1))


def right_three(table):
    high, low = host_split(table)
    return jnp.asarray(np.concatenate([high, high, low], 0))


def split(values):
    high = values.astype(BF16)
    low = (values - high.astype(F32)).astype(BF16)
    return high, low


def dot(left, right):
    return jnp.dot(left, right, preferred_element_type=F32)


def dot_left3(left3, values):
    high, low = split(values)
    return dot(left3, jnp.concatenate([high, low, high], 0))


def dot_right3(values, right3):
    high, low = split(values)
    return dot(jnp.concatenate([high, low, high], 1), right3)


def gelu(t):
    return 0.5 * t * (1.0 + lax.erf(t * np.float32(np.sqrt(0.5))))


def whole():
    return pl.BlockSpec(memory_space=pltpu.VMEM)


def forward_kernel(f_ref, ty_ref, tz_ref, out_ref, grown_ref):
    step = pl.program_id(0)
    block, local_x, cells_y, cells_z = f_ref.shape
    modes = ty_ref.shape[0] // 2
    n = out_ref.shape[0]
    per = modes // n
    rows = grown_ref.shape[0] // modes
    channels = rows // local_x
    half = channels // 2
    for c in range(block):
        wide = jnp.concatenate([f_ref[c, x] for x in range(local_x)], 1)
        high, low = split(wide)
        both = dot(ty_ref[...], jnp.concatenate([high, low], 0))
        both = both[:modes] + both[modes:]
        for x in range(local_x):
            grown_ref[pl.ds(x * channels + step * block + c, modes, stride=rows), :] = both[
                :, x * cells_z : (x + 1) * cells_z
            ]

    @pl.when(step == pl.num_programs(0) - 1)
    def _():
        lane = lax.broadcasted_iota(jnp.int32, (3 * half, 128), 1) // 32

        def owner(a, carry):
            at = pl.multiple_of(a * per * rows, 8)
            done = dot_right3(grown_ref[pl.ds(at, per * rows), :], tz_ref[...])
            total = jnp.concatenate([done[g * rows + 3 * half : (g + 1) * rows] for g in range(per)], 0)
            for g in range(per):
                total = jnp.where(lane == g, done[g * rows : g * rows + 3 * half], total)
            out_ref[a] = total
            return carry

        lax.fori_loop(0, n, owner, 0)


def forward_fine(features, modes_y, modes_z, n):
    channels, local_x, cells_y, cells_z = features.shape
    block = 4
    ty = left_rows(host_table(modes_y, cells_y))
    tz = right_three(np.tile(host_table(modes_z, cells_z).T, (1, 4)))
    shape = (n, modes_y // n * channels // 2, 128)
    return pl.pallas_call(
        forward_kernel,
        grid=(channels // block,),
        out_shape=jax.ShapeDtypeStruct(shape, F32),
        in_specs=[
            pl.BlockSpec((block, local_x, cells_y, cells_z), lambda h: (h, 0, 0, 0)),
            pl.BlockSpec(ty.shape, lambda h: (0, 0)),
            pl.BlockSpec(tz.shape, lambda h: (0, 0)),
        ],
        out_specs=pl.BlockSpec(shape, lambda h: (0, 0, 0)),
        scratch_shapes=[pltpu.VMEM((modes_y * local_x * channels, cells_z), F32)],
        name="forward_fine",
    )(features, ty, tz)


def middle_kernel(
    slab_ref, f_ref, ty_ref, tz_ref, yc_ref, zc_ref, zp_ref,
    level_ref, pooled_ref, coarse_ref, spec_ref, sum_ref, grown_ref,
):
    channels, local_x, cells_y, cells_z = f_ref.shape
    modes_y = ty_ref.shape[1] // 3
    n = slab_ref.shape[0]
    per = modes_y // n
    half = channels // 2
    rows = 2 * channels
    lane = lax.broadcasted_iota(jnp.int32, (rows, 128), 1) // 32
    tail = lax.broadcasted_iota(jnp.int32, (rows, 128), 0) >= 3 * half

    def inverse(a, carry):
        lefts = []
        for g in range(per):
            value = jnp.concatenate([slab_ref[a], slab_ref[a, g * half : (g + 1) * half]], 0)
            lefts.append(jnp.where(lane == jnp.where(tail, 3, g), value, 0.0))
        done = dot_right3(jnp.concatenate(lefts, 0), tz_ref[...])
        grown_ref[pl.ds(pl.multiple_of(a * per * rows, 8), per * rows), :] = done
        return carry

    lax.fori_loop(0, n, inverse, 0)

    def inverse_y(o, carry):
        wide = jnp.concatenate(
            [grown_ref[pl.ds(x * channels + o, modes_y, stride=rows), :] for x in range(local_x)], 1
        )
        done = dot_left3(ty_ref[...], wide)
        for x in range(local_x):
            spec_ref[o, x] = done[:, x * cells_z : (x + 1) * cells_z]
        return carry

    lax.fori_loop(0, channels, inverse_y, 0, unroll=4)

    def block(o, carry):
        level = [gelu(f_ref[o, x] + spec_ref[o, x]) for x in range(local_x)]
        for x in range(local_x):
            level_ref[o, x] = level[x]
        sum_ref[o] = level[0] + level[1]
        return carry

    lax.fori_loop(0, channels, block, 0)

    half_y = cells_y // 2
    modes_c = yc_ref.shape[0] // 2 - half_y
    parts = zc_ref.shape[1] // 128
    coarse_chunks = coarse_ref.shape[0] // (modes_c * parts)
    coarse_per = channels // coarse_chunks
    coarse_lane = (
        lax.broadcasted_iota(jnp.int32, (modes_c, parts * 128), 1) // (128 // coarse_per) % coarse_per
    )
    rows = modes_c + half_y

    def coarse(h, carry):
        total = jnp.zeros((modes_c, parts * 128), F32)
        for pair in range(coarse_per // 2):
            first = h * coarse_per + pair * 2
            wide = jnp.concatenate([sum_ref[first], sum_ref[first + 1]], 1)
            high, low = split(wide)
            both = dot(yc_ref[...], jnp.concatenate([high, low], 0))
            both = both[:rows] + both[rows:]
            modal = jnp.concatenate([both[half_y:, :128], both[half_y:, 128:]], 0)
            done = dot_right3(modal, zc_ref[...])
            for k in range(2):
                total = jnp.where(
                    coarse_lane == pair * 2 + k, done[k * modes_c : (k + 1) * modes_c], total
                )
            flat = jnp.concatenate([both[:half_y, :128], both[:half_y, 128:]], 0)
            high, low = split(flat)
            mean = dot(jnp.concatenate([high, low], 1), zp_ref[...])
            pooled_ref[first] = mean[:half_y]
            pooled_ref[first + 1] = mean[half_y:]
        for p in range(parts):
            coarse_ref[pl.ds(p * coarse_chunks + h, modes_c, stride=parts * coarse_chunks), :] = total[
                :, p * 128 : (p + 1) * 128
            ]
        return carry

    lax.fori_loop(0, coarse_chunks, coarse, 0)


def widen(matrix_ref, targets):
    channels = matrix_ref.shape[0]
    size = channels * 8
    row = lax.broadcasted_iota(jnp.int32, (size, channels), 0) // 8
    pick = (row == lax.broadcasted_iota(jnp.int32, (size, channels), 1)).astype(F32).astype(BF16)
    col = lax.broadcasted_iota(jnp.int32, (channels, size), 1) // 8
    place = (col == lax.broadcasted_iota(jnp.int32, (channels, size), 0)).astype(F32).astype(BF16)
    left = lax.broadcasted_iota(jnp.int32, (size, size), 0) % 8
    right = lax.broadcasted_iota(jnp.int32, (size, size), 1) % 8
    for part, spots in zip(split(matrix_ref[...]), ((0, 1), (2,))):
        grown = lax.dot_general(pick, part, (((1,), (1,)), ((), ())), preferred_element_type=F32)
        grown = dot(grown.astype(BF16), place)
        for ref, at, rule in targets:
            value = jnp.where(rule(left, right), grown, 0.0).astype(BF16)
            for spot in spots:
                ref[at : at + size, spot * size : (spot + 1) * size] = value


def same(left, right):
    return left == right


def load_block(ref, at):
    channels, local_x, _, cells_z = ref.shape
    return jnp.concatenate([ref[:, x, at, :].reshape(channels * 8, cells_z) for x in range(local_x)], 1)


def store_block(ref, at, value):
    channels, local_x, _, cells_z = ref.shape
    for x in range(local_x):
        ref[:, x, at, :] = value[:, x * cells_z : (x + 1) * cells_z].reshape(channels, 8, cells_z)


def greet(n):
    me = lax.axis_index("gx")
    barrier = pltpu.get_barrier_semaphore()
    for d in range(1, n):
        pl.semaphore_signal(barrier, 1, device_id={"gx": lax.rem(me + d, n)}, device_id_type=MESH)
    pl.semaphore_wait(barrier, n - 1)


def swap(n, source, target, send_sem, recv_sem, own_sem, work):
    me = lax.axis_index("gx")
    copies = []
    for d in range(1, n):
        peer = lax.rem(me + d, n)
        copy = pltpu.make_async_remote_copy(
            src_ref=source.at[peer],
            dst_ref=target.at[me],
            send_sem=send_sem.at[d],
            recv_sem=recv_sem.at[d],
            device_id={"gx": peer},
            device_id_type=MESH,
        )
        copy.start()
        copies.append(copy)
    own = pltpu.make_async_copy(source.at[me], target.at[me], own_sem)
    own.start()
    work()
    for copy in copies:
        copy.wait()
    own.wait()


def coarse_out_kernel(
    n, tx, in_ref, f_ref, level_ref, wide_ref, out_ref, base_ref, stage, got, send_sem, recv_sem, own_sem
):
    rows = stage.shape[1]
    for a in range(n):
        stage[a] = in_ref[a * rows : (a + 1) * rows]
    greet(n)

    def work():
        def block(b, carry):
            at = pl.ds(pl.multiple_of(b * 8, 8), 8)
            done = dot_left3(wide_ref[...], load_block(level_ref, at))
            store_block(base_ref, at, load_block(f_ref, at) + done)
            return carry

        lax.fori_loop(0, f_ref.shape[2] // 8, block, 0)

    swap(n, stage, got, send_sem, recv_sem, own_sem, work)
    for k in range(out_ref.shape[0]):
        out_ref[k] = sum(got[a] * np.float32(tx[k, a]) for a in range(n))


def coarse_back_kernel(
    n, tx, in_ref, pooled_ref, wide_ref, out_ref, lifted_ref, stage, got, send_sem, recv_sem, own_sem
):
    rows = stage.shape[1]
    for a in range(n):
        stage[a] = sum(in_ref[k] * np.float32(tx[k, a]) for k in range(in_ref.shape[0]))
    greet(n)
    channels, half_y, _ = pooled_ref.shape

    def work():
        def block(g, carry):
            at = [pl.ds(pl.multiple_of(g * 16 + 8 * k, 8), 8) for k in range(2)]
            pooled = jnp.concatenate([pooled_ref[:, a, :].reshape(channels * 8, 128) for a in at], 1)
            done = dot_left3(wide_ref[...], pooled)
            for k in range(2):
                lifted_ref[:, at[k], :] = done[:, k * 128 : (k + 1) * 128].reshape(channels, 8, 128)
            return carry

        lax.fori_loop(0, half_y // 16, block, 0)

    swap(n, stage, got, send_sem, recv_sem, own_sem, work)
    for a in range(n):
        out_ref[a * rows : (a + 1) * rows] = got[a]


def coarse_call(kernel, n, tx, rows, number, shapes, *values):
    return pl.pallas_call(
        functools.partial(kernel, n, tx),
        out_shape=tuple(jax.ShapeDtypeStruct(shape, F32) for shape in shapes),
        in_specs=[whole()] * len(values),
        out_specs=(whole(),) * len(shapes),
        scratch_shapes=[
            pltpu.VMEM((n, rows, 128), F32),
            pltpu.VMEM((n, rows, 128), F32),
            pltpu.SemaphoreType.DMA((n,)),
            pltpu.SemaphoreType.DMA((n,)),
            pltpu.SemaphoreType.DMA,
        ],
        compiler_params=pltpu.CompilerParams(collective_id=number, has_side_effects=True),
        name=kernel.__name__,
    )(*values)


def mix_kernel(
    n, tx, wire_ref, w_hbm, f_ref, lift_ref, middle_ref, project_ref,
    out_ref, lifted_ref, middle_wide, proj_wide, final_wide, lift_wide, got, w_ref, modal, mixed, back,
    send_one, recv_one, send_two, recv_two, own_sem, w_sem,
):
    modes_x, channels, _, owned = w_ref.shape
    half = channels // 2
    fetch = pltpu.make_async_copy(w_hbm, w_ref, w_sem)
    fetch.start()
    greet(n)

    def lift():
        widen(lift_ref, ((lift_wide, 0, same),))

        def block(b, carry):
            at = pl.ds(pl.multiple_of(b * 8, 8), 8)
            store_block(lifted_ref, at, dot_left3(lift_wide[...], load_block(f_ref, at)))
            return carry

        lax.fori_loop(0, f_ref.shape[2] // 8, block, 0)

    swap(n, wire_ref, got, send_one, recv_one, own_sem.at[0], lift)
    fetch.wait()
    lane = lax.broadcasted_iota(jnp.int32, (half, 128), 1)
    for k in range(modes_x):
        first = sum(got[a, :channels] * np.float32(tx[k, a, 0]) for a in range(n))
        second = sum(got[a] * np.float32(tx[k, a, 1]) for a in range(n))
        extra = jnp.zeros((half, 128), F32)
        for g in range(3):
            piece = pltpu.roll(second[g * half : (g + 1) * half], 32 * (g + 1), 1)
            extra = jnp.where(lane // 32 == g, piece, extra)
        total = first + jnp.concatenate([second[channels:], extra], 0)
        modal[k] = total.astype(BF16).astype(F32)
    mixed[...] = jnp.zeros_like(mixed)

    def mode(k, carry):
        total = jnp.zeros((channels, owned), F32)
        for c in range(channels):
            total += modal[k, c : c + 1, :owned] * w_ref[k, c].astype(F32)
        mixed[k, :, :owned] = total
        return carry

    lax.fori_loop(0, modes_x, mode, 0)
    wide = lax.broadcasted_iota(jnp.int32, (3 * half, 128), 1)
    for a in range(n):
        first = sum(mixed[k] * np.float32(tx[k, a, 0]) for k in range(modes_x))
        second = sum(mixed[k] * np.float32(tx[k, a, 1]) for k in range(modes_x))
        rolled = jnp.concatenate([pltpu.roll(second[half:], 96 - 32 * g, 1) for g in range(3)], 0)
        back[a] = jnp.where(wide < 96, jnp.concatenate([first, second[:half]], 0), rolled)

    def matrices():
        size = channels * 8
        widen(middle_ref, ((middle_wide, 0, same),))
        widen(
            project_ref,
            (
                (proj_wide, 0, same),
                (final_wide, 0, lambda left, right: left // 2 == right),
                (final_wide, size, lambda left, right: left // 2 + 4 == right),
            ),
        )

    swap(n, back, out_ref, send_two, recv_two, own_sem.at[1], matrices)


def mix_fine(wire, weights, features, matrices, tx, n):
    turned = jnp.transpose(weights, (1, 2, 3, 0))
    modes_x, channels = turned.shape[:2]
    size = channels * 8
    wide = jax.ShapeDtypeStruct((size, 3 * size), BF16)
    return pl.pallas_call(
        functools.partial(mix_kernel, n, tx),
        out_shape=(
            jax.ShapeDtypeStruct(wire.shape, F32),
            jax.ShapeDtypeStruct(features.shape, F32),
            wide,
            wide,
            jax.ShapeDtypeStruct((2 * size, 3 * size), BF16),
        ),
        in_specs=[whole(), pl.BlockSpec(memory_space=pl.ANY)] + [whole()] * 4,
        out_specs=(whole(),) * 5,
        scratch_shapes=[
            pltpu.VMEM(wide.shape, BF16),
            pltpu.VMEM(wire.shape, F32),
            pltpu.VMEM(turned.shape, BF16),
            pltpu.VMEM((modes_x, channels, 128), F32),
            pltpu.VMEM((modes_x, channels, 128), F32),
            pltpu.VMEM(wire.shape, F32),
        ]
        + [pltpu.SemaphoreType.DMA((n,))] * 4
        + [pltpu.SemaphoreType.DMA((2,)), pltpu.SemaphoreType.DMA],
        compiler_params=pltpu.CompilerParams(collective_id=0, has_side_effects=True),
        name="mix_fine",
    )(wire, turned, features, *matrices)


def final_kernel(
    slab_ref, pooled_ref, base_ref, ty_ref, tz_ref, proj_ref, out_ref, spec_ref
):
    channels, half_y, _ = pooled_ref.shape
    local_x = base_ref.shape[1]
    modes = ty_ref.shape[1] // 3
    rows_per_mode = slab_ref.shape[0] // modes
    parts = tz_ref.shape[0] // (3 * 128)
    chunks = rows_per_mode // parts
    per_row = channels // chunks
    stacked = []
    for h in range(chunks):
        wide = jnp.concatenate(
            [slab_ref[pl.ds(p * chunks + h, modes, stride=rows_per_mode), :] for p in range(parts)], 1
        )
        stacked.append(dot_left3(ty_ref[...], wide))
    grown = jnp.concatenate(stacked, 0)
    high, low = split(grown)
    left = jnp.concatenate([high, low, high], 1)
    lane = lax.broadcasted_iota(jnp.int32, left.shape, 1) // (128 // per_row) % per_row

    for c in range(per_row):
        done = dot(jnp.where(lane == c, left, jnp.zeros_like(left)), tz_ref[...])
        for h in range(chunks):
            spec_ref[h * per_row + c] = done[h * half_y : (h + 1) * half_y]

    def block(g, carry):
        at = [pl.ds(pl.multiple_of(g * 16 + 8 * k, 8), 8) for k in range(2)]
        pooled = jnp.concatenate([pooled_ref[:, a, :].reshape(channels * 8, 128) for a in at], 1)
        spectral = jnp.concatenate([spec_ref[:, a, :].reshape(channels * 8, 128) for a in at], 1)
        level = gelu(pooled + spectral)
        added = dot_left3(proj_ref[...], level)
        for k in range(2):
            for b in range(2):
                piece = added[b * channels * 8 : (b + 1) * channels * 8, k * 128 : (k + 1) * 128]
                piece = piece.reshape(channels, 8, 128)
                rows = pl.ds(pl.multiple_of(g * 32 + 16 * k + 8 * b, 8), 8)
                for x in range(local_x):
                    out_ref[:, x, rows, :] = base_ref[:, x, rows, :] + piece
        return carry

    lax.fori_loop(0, half_y // 16, block, 0)


def on_device(features, fine_weights, middle_weights, lift_fine, lift_middle, project_out):
    channels, local_x, cells_y, cells_z = features.shape
    n = lax.axis_size("gx")
    owned = fine_weights.shape[0]
    owned_c = middle_weights.shape[0]
    half_ky, half_kz = KY // 2, KZ // 2
    narrow = 8
    fits = (
        owned == 3 * KZ
        and KZ == 32
        and KY == 3 * n
        and owned_c % narrow == 0
        and local_x == 2
        and cells_z == 128
        and cells_y % 32 == 0
        and channels % 16 == 0
    )
    if not fits:
        return general_device(
            features, fine_weights, middle_weights, lift_fine, lift_middle, project_out
        )
    modes_x = fine_weights.shape[1]
    modes_c = middle_weights.shape[1]
    tx = np.asarray(host_table(modes_x, local_x * n), np.float32).reshape(modes_x, n, local_x)
    txc = np.asarray(host_table(modes_c, n), np.float32)
    wire = forward_fine(features, KY, KZ, n)
    slab, lifted, liftm, proj, projm = mix_fine(
        wire, fine_weights, features, (lift_fine, lift_middle, project_out), tx, n
    )

    half_y, half_z = cells_y // 2, cells_z // 2
    pool_y = np.repeat(np.eye(half_y), 2, axis=1) * 0.5
    pool_z = np.repeat(np.eye(half_z), 2, axis=1) * 0.25
    ty_c = host_table(half_ky, half_y)
    tz_c = host_table(half_kz, half_z)
    parts = half_kz // narrow
    per_c = 128 // narrow
    chunks_c = channels // per_c
    yc = left_rows(np.concatenate([pool_y, ty_c @ pool_y], 0))
    zc_full = (tz_c @ pool_z).T.reshape(cells_z, parts, 1, narrow)
    zc = right_three(np.broadcast_to(zc_full, (cells_z, parts, per_c, narrow)).reshape(cells_z, -1))
    zp = np.repeat(pool_z, 2, axis=0).T
    zp = np.asarray(zp, jnp.bfloat16)
    zp = jnp.asarray(np.concatenate([zp, zp], 0))
    ty_i = left_three(host_table(KY, cells_y).T)
    tz_i = right_three(np.tile(host_table(KZ, cells_z), (4, 1)))
    level, pooled, coarse = pl.pallas_call(
        middle_kernel,
        out_shape=(
            jax.ShapeDtypeStruct(features.shape, F32),
            jax.ShapeDtypeStruct((channels, half_y, 128), F32),
            jax.ShapeDtypeStruct((half_ky * parts * chunks_c, 128), F32),
        ),
        in_specs=[whole()] * 7,
        out_specs=(whole(), whole(), whole()),
        scratch_shapes=[
            pltpu.VMEM(features.shape, F32),
            pltpu.VMEM((channels, cells_y, cells_z), F32),
            pltpu.VMEM((KY * local_x * channels, cells_z), F32),
        ],
        name="middle",
    )(slab, lifted, ty_i, tz_i, yc, zc, zp)

    count = owned_c // narrow
    rows = count * chunks_c
    modal, base = coarse_call(
        coarse_out_kernel, n, txc, rows, 1, ((modes_c, rows, 128), features.shape),
        coarse, features, level, proj,
    )
    modal = modal.reshape(modes_c, count, channels, narrow).transpose(1, 3, 0, 2)
    mixed = mix_modes(modal.reshape(owned_c, modes_c, channels), middle_weights)
    mixed = mixed.reshape(count, narrow, modes_c, channels).transpose(2, 0, 3, 1)
    slab, lifted = coarse_call(
        coarse_back_kernel, n, txc, rows, 2, ((n * rows, 128), pooled.shape),
        mixed.reshape(modes_c, rows, 128), pooled, liftm,
    )

    tyc_i = left_three(ty_c.T)
    grown = np.repeat(tz_c, 2, axis=1).reshape(parts, 1, narrow, cells_z)
    tzc_i = right_three(np.broadcast_to(grown, (parts, per_c, narrow, cells_z)).reshape(-1, cells_z))
    return pl.pallas_call(
        final_kernel,
        out_shape=jax.ShapeDtypeStruct(features.shape, F32),
        in_specs=[whole()] * 6,
        out_specs=whole(),
        scratch_shapes=[pltpu.VMEM((channels, half_y, 128), F32)],
        name="final",
    )(slab, lifted, base, tyc_i, tzc_i, projm)


def solution(mesh):
    in_specs = (
        P(None, ("groups", "gx"), None, None),
        P("gx", None, None, None),
        P("gx", None, None, None),
        P(),
        P(),
        P(),
    )
    out_specs = P(None, ("groups", "gx"), None, None)
    return jax.shard_map(
        on_device, mesh=mesh, in_specs=in_specs, out_specs=out_specs, check_vma=False
    )
```

```python
import functools

import jax
import jax.numpy as jnp
import numpy as np
from jax import lax
from jax.experimental import pallas as pl
from jax.experimental.pallas import tpu as pltpu
from jax.sharding import PartitionSpec as P

KY = 48
KZ = 32


HIGHEST = lax.Precision.HIGHEST


def cosine_table(modes_kept, length, columns):
    orders = jnp.arange(modes_kept, dtype=jnp.int32)[:, None]
    points = jnp.arange(columns, dtype=jnp.int32)[None, :]
    phase = orders * (2 * points + 1) % (4 * length)
    angle = jnp.pi / (2 * length) * phase.astype(jnp.float32)
    scales = jnp.where(
        orders == 0, jnp.sqrt(jnp.float32(1.0 / length)), jnp.sqrt(jnp.float32(2.0 / length))
    )
    return scales * jnp.cos(angle)


def forward_yz(values, modes_y, modes_z):
    channels, local_x, cells_y, cells_z = values.shape
    table_z = cosine_table(modes_z, cells_z, cells_z)
    table_y = cosine_table(modes_y, cells_y, cells_y)
    along_z = jnp.einsum("cxyz,jz->cxyj", values, table_z, precision=HIGHEST)
    both = jnp.einsum("cxyj,iy->ijxc", along_z, table_y, precision=HIGHEST)
    return both.reshape(modes_y * modes_z, local_x, channels)


def inverse_yz(coeffs, modes_y, modes_z, cells_y, cells_z):
    total, local_x, channels = coeffs.shape
    shaped = coeffs.reshape(modes_y, modes_z, local_x, channels)
    table_z = cosine_table(modes_z, cells_z, cells_z)
    table_y = cosine_table(modes_y, cells_y, cells_y)
    along_y = jnp.einsum("ijxc,iy->jxcy", shaped, table_y, precision=HIGHEST)
    return jnp.einsum("jxcy,jz->cxyz", along_y, table_z, precision=HIGHEST)


def mix_modes(modal, weights):
    return jnp.einsum(
        "mkc,mkco->mko", modal.astype(jnp.bfloat16), weights, preferred_element_type=jnp.float32
    )


def pointwise(values, matrix):
    return jnp.einsum("cxyz,co->oxyz", values, matrix, precision=HIGHEST)


def coarsen(values):
    channels, cells_x, cells_y, cells_z = values.shape
    shaped = values.reshape(channels, cells_x // 2, 2, cells_y // 2, 2, cells_z // 2, 2)
    return jnp.mean(shaped, axis=(2, 4, 6))


def refine(values):
    return jnp.repeat(jnp.repeat(jnp.repeat(values, 2, axis=1), 2, axis=2), 2, axis=3)


def general_device(features, fine_weights, middle_weights, lift_fine, lift_middle, project_out):
    channels, local_x, cells_y, cells_z = features.shape
    group_size = lax.axis_size("gx")
    cells_x = local_x * group_size
    modes_x = fine_weights.shape[1]
    coeffs = forward_yz(features, KY, KZ)
    table_x = cosine_table(modes_x, cells_x, cells_x)
    owned_pairs = coeffs.shape[0] // group_size
    grouped = coeffs.reshape(group_size, owned_pairs, local_x, channels)
    modal = jnp.einsum(
        "amxc,kx->mkc",
        lax.all_to_all(grouped, "gx", split_axis=0, concat_axis=2, tiled=True),
        table_x,
        precision=HIGHEST,
    )
    mixed = mix_modes(modal, fine_weights)
    back = jnp.einsum("mkc,kx->mxc", mixed, table_x, precision=HIGHEST)
    slabs = lax.all_to_all(back, "gx", split_axis=1, concat_axis=0, tiled=True)
    level_one = jax.nn.gelu(
        inverse_yz(slabs, KY, KZ, cells_y, cells_z) + pointwise(features, lift_fine),
        approximate=False,
    )
    pooled = coarsen(level_one)
    half_x = local_x // 2
    half_ky = KY // 2
    half_kz = KZ // 2
    half_modes = middle_weights.shape[1]
    coarse_x = half_x * group_size
    coarse_coeffs = forward_yz(pooled, half_ky, half_kz)
    coarse_pencils = lax.all_to_all(coarse_coeffs, "gx", split_axis=0, concat_axis=1, tiled=True)
    coarse_table = cosine_table(half_modes, coarse_x, coarse_x)
    coarse_modal = jnp.einsum("mxc,kx->mkc", coarse_pencils, coarse_table, precision=HIGHEST)
    coarse_mixed = mix_modes(coarse_modal, middle_weights)
    coarse_back = jnp.einsum("mkc,kx->mxc", coarse_mixed, coarse_table, precision=HIGHEST)
    coarse_slabs = lax.all_to_all(coarse_back, "gx", split_axis=1, concat_axis=0, tiled=True)
    level_two = jax.nn.gelu(
        inverse_yz(coarse_slabs, half_ky, half_kz, cells_y // 2, cells_z // 2)
        + pointwise(pooled, lift_middle),
        approximate=False,
    )
    return features + pointwise(level_one + refine(level_two), project_out)


BF16 = jnp.bfloat16
MESH = pl.DeviceIdType.MESH
F32 = jnp.float32


def host_table(modes_kept, length):
    orders = np.arange(modes_kept)[:, None]
    points = np.arange(length)[None, :]
    scales = np.where(orders == 0, np.sqrt(1.0 / length), np.sqrt(2.0 / length))
    return scales * np.cos(np.pi * orders * (2 * points + 1) / (2 * length))


def host_split(table):
    table = np.asarray(table, np.float32)
    high = table.astype(jnp.bfloat16)
    low = (table - high.astype(np.float32)).astype(jnp.bfloat16)
    return high, low


def left_rows(table):
    high, low = host_split(table)
    return jnp.asarray(
        np.concatenate([np.concatenate([high, high], 1), np.concatenate([low, low], 1)], 0)
    )


def left_three(table):
    high, low = host_split(table)
    return jnp.asarray(np.concatenate([high, high, low], 1))


def right_three(table):
    high, low = host_split(table)
    return jnp.asarray(np.concatenate([high, high, low], 0))


def split(values):
    high = values.astype(BF16)
    low = (values - high.astype(F32)).astype(BF16)
    return high, low


def dot(left, right):
    return jnp.dot(left, right, preferred_element_type=F32)


def dot_left3(left3, values):
    high, low = split(values)
    return dot(left3, jnp.concatenate([high, low, high], 0))


def dot_right3(values, right3):
    high, low = split(values)
    return dot(jnp.concatenate([high, low, high], 1), right3)


def gelu(t):
    return 0.5 * t * (1.0 + lax.erf(t * np.float32(np.sqrt(0.5))))


def far():
    return pl.BlockSpec(memory_space=pl.ANY)


def whole():
    return pl.BlockSpec(memory_space=pltpu.VMEM)


def forward_kernel(f_ref, ty_ref, tz_ref, out_ref, grown_ref):
    step = pl.program_id(0)
    block, local_x, cells_y, cells_z = f_ref.shape
    modes = ty_ref.shape[0] // 2
    n = out_ref.shape[0]
    per = modes // n
    rows = grown_ref.shape[0] // modes
    channels = rows // local_x
    half = channels // 2
    for c in range(block):
        wide = jnp.concatenate([f_ref[c, x] for x in range(local_x)], 1)
        high, low = split(wide)
        both = dot(ty_ref[...], jnp.concatenate([high, low], 0))
        both = both[:modes] + both[modes:]
        for x in range(local_x):
            grown_ref[pl.ds(x * channels + step * block + c, modes, stride=rows), :] = both[
                :, x * cells_z : (x + 1) * cells_z
            ]

    @pl.when(step == pl.num_programs(0) - 1)
    def _():
        lane = lax.broadcasted_iota(jnp.int32, (3 * half, 128), 1) // 32

        def owner(a, carry):
            at = pl.multiple_of(a * per * rows, 8)
            done = dot_right3(grown_ref[pl.ds(at, per * rows), :], tz_ref[...])
            total = jnp.concatenate([done[g * rows + 3 * half : (g + 1) * rows] for g in range(per)], 0)
            for g in range(per):
                total = jnp.where(lane == g, done[g * rows : g * rows + 3 * half], total)
            out_ref[a] = total
            return carry

        lax.fori_loop(0, n, owner, 0)


def forward_fine(features, modes_y, modes_z, n):
    channels, local_x, cells_y, cells_z = features.shape
    block = 4
    ty = left_rows(host_table(modes_y, cells_y))
    tz = right_three(np.tile(host_table(modes_z, cells_z).T, (1, 4)))
    shape = (n, modes_y // n * channels // 2, 128)
    return pl.pallas_call(
        forward_kernel,
        grid=(channels // block,),
        out_shape=jax.ShapeDtypeStruct(shape, F32),
        in_specs=[
            pl.BlockSpec((block, local_x, cells_y, cells_z), lambda h: (h, 0, 0, 0)),
            pl.BlockSpec(ty.shape, lambda h: (0, 0)),
            pl.BlockSpec(tz.shape, lambda h: (0, 0)),
        ],
        out_specs=pl.BlockSpec(shape, lambda h: (0, 0, 0)),
        scratch_shapes=[pltpu.VMEM((modes_y * local_x * channels, cells_z), F32)],
        name="forward_fine",
    )(features, ty, tz)


def middle_kernel(
    slab_ref, f_hbm, ty_ref, tz_ref, yc_ref, zc_ref, zp_ref,
    level_hbm, pooled_ref, coarse_ref, spec_ref, sum_ref, grown_ref, f_ref, move_sem,
):
    load = pltpu.make_async_copy(f_hbm, f_ref, move_sem.at[0])
    load.start()
    save = pltpu.make_async_copy(f_ref, level_hbm, move_sem.at[1])
    channels, local_x, cells_y, cells_z = f_ref.shape
    modes_y = ty_ref.shape[1] // 3
    n = slab_ref.shape[0]
    per = modes_y // n
    half = channels // 2
    rows = 2 * channels
    lane = lax.broadcasted_iota(jnp.int32, (rows, 128), 1) // 32
    tail = lax.broadcasted_iota(jnp.int32, (rows, 128), 0) >= 3 * half

    def inverse(a, carry):
        lefts = []
        for g in range(per):
            value = jnp.concatenate([slab_ref[a], slab_ref[a, g * half : (g + 1) * half]], 0)
            lefts.append(jnp.where(lane == jnp.where(tail, 3, g), value, 0.0))
        done = dot_right3(jnp.concatenate(lefts, 0), tz_ref[...])
        grown_ref[pl.ds(pl.multiple_of(a * per * rows, 8), per * rows), :] = done
        return carry

    lax.fori_loop(0, n, inverse, 0)

    def inverse_y(o, carry):
        wide = jnp.concatenate(
            [grown_ref[pl.ds(x * channels + o, modes_y, stride=rows), :] for x in range(local_x)], 1
        )
        done = dot_left3(ty_ref[...], wide)
        for x in range(local_x):
            spec_ref[o, x] = done[:, x * cells_z : (x + 1) * cells_z]
        return carry

    lax.fori_loop(0, channels, inverse_y, 0, unroll=4)

    load.wait()

    def block(o, carry):
        level = [gelu(f_ref[o, x] + spec_ref[o, x]) for x in range(local_x)]
        for x in range(local_x):
            f_ref[o, x] = level[x]
        sum_ref[o] = level[0] + level[1]
        return carry

    lax.fori_loop(0, channels, block, 0)
    save.start()

    half_y = cells_y // 2
    modes_c = yc_ref.shape[0] // 2 - half_y
    parts = zc_ref.shape[1] // 128
    coarse_chunks = coarse_ref.shape[0] // (modes_c * parts)
    coarse_per = channels // coarse_chunks
    coarse_lane = (
        lax.broadcasted_iota(jnp.int32, (modes_c, parts * 128), 1) // (128 // coarse_per) % coarse_per
    )
    rows = modes_c + half_y

    def coarse(h, carry):
        total = jnp.zeros((modes_c, parts * 128), F32)
        for pair in range(coarse_per // 2):
            first = h * coarse_per + pair * 2
            wide = jnp.concatenate([sum_ref[first], sum_ref[first + 1]], 1)
            high, low = split(wide)
            both = dot(yc_ref[...], jnp.concatenate([high, low], 0))
            both = both[:rows] + both[rows:]
            modal = jnp.concatenate([both[half_y:, :128], both[half_y:, 128:]], 0)
            done = dot_right3(modal, zc_ref[...])
            for k in range(2):
                total = jnp.where(
                    coarse_lane == pair * 2 + k, done[k * modes_c : (k + 1) * modes_c], total
                )
            flat = jnp.concatenate([both[:half_y, :128], both[:half_y, 128:]], 0)
            high, low = split(flat)
            mean = dot(jnp.concatenate([high, low], 1), zp_ref[...])
            pooled_ref[first] = mean[:half_y]
            pooled_ref[first + 1] = mean[half_y:]
        for p in range(parts):
            coarse_ref[pl.ds(p * coarse_chunks + h, modes_c, stride=parts * coarse_chunks), :] = total[
                :, p * 128 : (p + 1) * 128
            ]
        return carry

    lax.fori_loop(0, coarse_chunks, coarse, 0)
    save.wait()


def widen(matrix_ref, targets):
    channels = matrix_ref.shape[0]
    size = channels * 8
    row = lax.broadcasted_iota(jnp.int32, (size, channels), 0) // 8
    pick = (row == lax.broadcasted_iota(jnp.int32, (size, channels), 1)).astype(F32).astype(BF16)
    col = lax.broadcasted_iota(jnp.int32, (channels, size), 1) // 8
    place = (col == lax.broadcasted_iota(jnp.int32, (channels, size), 0)).astype(F32).astype(BF16)
    left = lax.broadcasted_iota(jnp.int32, (size, size), 0) % 8
    right = lax.broadcasted_iota(jnp.int32, (size, size), 1) % 8
    for part, spots in zip(split(matrix_ref[...]), ((0, 1), (2,))):
        grown = lax.dot_general(pick, part, (((1,), (1,)), ((), ())), preferred_element_type=F32)
        grown = dot(grown.astype(BF16), place)
        for ref, at, rule in targets:
            value = jnp.where(rule(left, right), grown, 0.0).astype(BF16)
            for spot in spots:
                ref[at : at + size, spot * size : (spot + 1) * size] = value


def same(left, right):
    return left == right


def load_block(ref, at):
    channels, local_x, _, cells_z = ref.shape
    return jnp.concatenate([ref[:, x, at, :].reshape(channels * 8, cells_z) for x in range(local_x)], 1)


def store_block(ref, at, value):
    channels, local_x, _, cells_z = ref.shape
    for x in range(local_x):
        ref[:, x, at, :] = value[:, x * cells_z : (x + 1) * cells_z].reshape(channels, 8, cells_z)


def greet(n):
    me = lax.axis_index("gx")
    barrier = pltpu.get_barrier_semaphore()
    for d in range(1, n):
        pl.semaphore_signal(barrier, 1, device_id={"gx": lax.rem(me + d, n)}, device_id_type=MESH)
    pl.semaphore_wait(barrier, n - 1)


def swap(n, source, target, send_sem, recv_sem, own_sem, work):
    me = lax.axis_index("gx")
    copies = []
    for d in range(1, n):
        peer = lax.rem(me + d, n)
        copy = pltpu.make_async_remote_copy(
            src_ref=source.at[peer],
            dst_ref=target.at[me],
            send_sem=send_sem.at[d],
            recv_sem=recv_sem.at[d],
            device_id={"gx": peer},
            device_id_type=MESH,
        )
        copy.start()
        copies.append(copy)
    own = pltpu.make_async_copy(source.at[me], target.at[me], own_sem)
    own.start()
    work()
    for copy in copies:
        copy.wait()
    own.wait()


class Half:
    def __init__(self, side, f_hbm, level_hbm, wide_ref, base_hbm, f_ref, level_ref, sem):
        rows = f_ref.shape[2]
        at = pl.ds(side * rows, rows)
        self.loads = [
            pltpu.make_async_copy(f_hbm.at[:, :, at, :], f_ref, sem.at[0]),
            pltpu.make_async_copy(level_hbm.at[:, :, at, :], level_ref, sem.at[1]),
        ]
        self.save = pltpu.make_async_copy(f_ref, base_hbm, sem.at[2])
        self.refs = f_ref, level_ref, wide_ref

    def start(self):
        for load in self.loads:
            load.start()

    def work(self):
        f_ref, level_ref, wide_ref = self.refs
        for load in self.loads:
            load.wait()

        def block(b, carry):
            at = pl.ds(pl.multiple_of(b * 8, 8), 8)
            done = dot_left3(wide_ref[...], load_block(level_ref, at))
            store_block(f_ref, at, load_block(f_ref, at) + done)
            return carry

        lax.fori_loop(0, f_ref.shape[2] // 8, block, 0)
        self.save.start()


def coarse_out_kernel(
    n, tx, in_ref, f_hbm, level_hbm, wide_ref, out_ref, base_hbm,
    stage, got, send_sem, recv_sem, own_sem, f_ref, level_ref, move_sem,
):
    half = Half(0, f_hbm, level_hbm, wide_ref, base_hbm, f_ref, level_ref, move_sem)
    half.start()
    rows = stage.shape[1]
    for a in range(n):
        stage[a] = in_ref[a * rows : (a + 1) * rows]
    greet(n)
    swap(n, stage, got, send_sem, recv_sem, own_sem, half.work)
    for k in range(out_ref.shape[0]):
        out_ref[k] = sum(got[a] * np.float32(tx[k, a]) for a in range(n))
    half.save.wait()


def coarse_back_kernel(
    n, tx, in_ref, f_hbm, level_hbm, proj_ref, pooled_ref, wide_ref, out_ref, base_hbm, lifted_ref,
    stage, got, send_sem, recv_sem, own_sem, f_ref, level_ref, move_sem,
):
    half = Half(1, f_hbm, level_hbm, proj_ref, base_hbm, f_ref, level_ref, move_sem)
    half.start()
    rows = stage.shape[1]
    for a in range(n):
        stage[a] = sum(in_ref[k] * np.float32(tx[k, a]) for k in range(in_ref.shape[0]))
    greet(n)
    channels, half_y, _ = pooled_ref.shape

    def work():
        def block(g, carry):
            at = [pl.ds(pl.multiple_of(g * 16 + 8 * k, 8), 8) for k in range(2)]
            pooled = jnp.concatenate([pooled_ref[:, a, :].reshape(channels * 8, 128) for a in at], 1)
            done = dot_left3(wide_ref[...], pooled)
            for k in range(2):
                lifted_ref[:, at[k], :] = done[:, k * 128 : (k + 1) * 128].reshape(channels, 8, 128)
            return carry

        lax.fori_loop(0, half_y // 16, block, 0)
        half.work()

    swap(n, stage, got, send_sem, recv_sem, own_sem, work)
    for a in range(n):
        out_ref[a * rows : (a + 1) * rows] = got[a]
    half.save.wait()


def coarse_call(kernel, n, tx, rows, number, shapes, *values):
    channels, local_x, cells_y, cells_z = values[1].shape
    part = (channels, local_x, cells_y // 2, cells_z)
    shapes = (shapes[0], part) + tuple(shapes[1:])
    return pl.pallas_call(
        functools.partial(kernel, n, tx),
        out_shape=tuple(jax.ShapeDtypeStruct(shape, F32) for shape in shapes),
        in_specs=[whole(), far(), far()] + [whole()] * (len(values) - 3),
        out_specs=(whole(), far()) + (whole(),) * (len(shapes) - 2),
        scratch_shapes=[
            pltpu.VMEM((n, rows, 128), F32),
            pltpu.VMEM((n, rows, 128), F32),
            pltpu.SemaphoreType.DMA((n,)),
            pltpu.SemaphoreType.DMA((n,)),
            pltpu.SemaphoreType.DMA,
            pltpu.VMEM(part, F32),
            pltpu.VMEM(part, F32),
            pltpu.SemaphoreType.DMA((3,)),
        ],
        compiler_params=pltpu.CompilerParams(collective_id=number, has_side_effects=True),
        name=kernel.__name__,
    )(*values)


def mix_kernel(
    n, tx, wire_ref, w_hbm, f_hbm, lift_ref, middle_ref, project_ref,
    out_ref, lifted_hbm, middle_wide, proj_wide, final_wide, f_ref, move_sem, lift_wide, got, w_ref, modal, mixed, back,
    send_one, recv_one, send_two, recv_two, own_sem, w_sem,
):
    modes_x, channels, _, owned = w_ref.shape
    half = channels // 2
    fetch = pltpu.make_async_copy(w_hbm, w_ref, w_sem)
    fetch.start()
    load = pltpu.make_async_copy(f_hbm, f_ref, move_sem.at[0])
    load.start()
    save = pltpu.make_async_copy(f_ref, lifted_hbm, move_sem.at[1])
    greet(n)

    def lift():
        widen(lift_ref, ((lift_wide, 0, same),))
        load.wait()

        def block(b, carry):
            at = pl.ds(pl.multiple_of(b * 8, 8), 8)
            store_block(f_ref, at, dot_left3(lift_wide[...], load_block(f_ref, at)))
            return carry

        lax.fori_loop(0, f_ref.shape[2] // 8, block, 0)
        save.start()

    swap(n, wire_ref, got, send_one, recv_one, own_sem.at[0], lift)
    fetch.wait()
    lane = lax.broadcasted_iota(jnp.int32, (half, 128), 1)
    for k in range(modes_x):
        first = sum(got[a, :channels] * np.float32(tx[k, a, 0]) for a in range(n))
        second = sum(got[a] * np.float32(tx[k, a, 1]) for a in range(n))
        extra = jnp.zeros((half, 128), F32)
        for g in range(3):
            piece = pltpu.roll(second[g * half : (g + 1) * half], 32 * (g + 1), 1)
            extra = jnp.where(lane // 32 == g, piece, extra)
        total = first + jnp.concatenate([second[channels:], extra], 0)
        modal[k] = total.astype(BF16).astype(F32)
    mixed[...] = jnp.zeros_like(mixed)

    def mode(k, carry):
        total = jnp.zeros((channels, owned), F32)
        for c in range(channels):
            total += modal[k, c : c + 1, :owned] * w_ref[k, c].astype(F32)
        mixed[k, :, :owned] = total
        return carry

    lax.fori_loop(0, modes_x, mode, 0)
    wide = lax.broadcasted_iota(jnp.int32, (3 * half, 128), 1)
    for a in range(n):
        first = sum(mixed[k] * np.float32(tx[k, a, 0]) for k in range(modes_x))
        second = sum(mixed[k] * np.float32(tx[k, a, 1]) for k in range(modes_x))
        rolled = jnp.concatenate([pltpu.roll(second[half:], 96 - 32 * g, 1) for g in range(3)], 0)
        back[a] = jnp.where(wide < 96, jnp.concatenate([first, second[:half]], 0), rolled)

    def matrices():
        size = channels * 8
        widen(middle_ref, ((middle_wide, 0, same),))
        widen(
            project_ref,
            (
                (proj_wide, 0, same),
                (final_wide, 0, lambda left, right: left // 2 == right),
                (final_wide, size, lambda left, right: left // 2 + 4 == right),
            ),
        )

    swap(n, back, out_ref, send_two, recv_two, own_sem.at[1], matrices)
    save.wait()


def mix_fine(wire, weights, features, matrices, tx, n):
    turned = jnp.transpose(weights, (1, 2, 3, 0))
    modes_x, channels = turned.shape[:2]
    size = channels * 8
    wide = jax.ShapeDtypeStruct((size, 3 * size), BF16)
    return pl.pallas_call(
        functools.partial(mix_kernel, n, tx),
        out_shape=(
            jax.ShapeDtypeStruct(wire.shape, F32),
            jax.ShapeDtypeStruct(features.shape, F32),
            wide,
            wide,
            jax.ShapeDtypeStruct((2 * size, 3 * size), BF16),
        ),
        in_specs=[whole(), far(), far()] + [whole()] * 3,
        out_specs=(whole(), far()) + (whole(),) * 3,
        scratch_shapes=[
            pltpu.VMEM(features.shape, F32),
            pltpu.SemaphoreType.DMA((2,)),
            pltpu.VMEM(wide.shape, BF16),
            pltpu.VMEM(wire.shape, F32),
            pltpu.VMEM(turned.shape, BF16),
            pltpu.VMEM((modes_x, channels, 128), F32),
            pltpu.VMEM((modes_x, channels, 128), F32),
            pltpu.VMEM(wire.shape, F32),
        ]
        + [pltpu.SemaphoreType.DMA((n,))] * 4
        + [pltpu.SemaphoreType.DMA((2,)), pltpu.SemaphoreType.DMA],
        compiler_params=pltpu.CompilerParams(collective_id=0, has_side_effects=True),
        name="mix_fine",
    )(wire, turned, features, *matrices)


def final_kernel(
    slab_ref, pooled_ref, low_hbm, high_hbm, ty_ref, tz_ref, proj_ref, out_hbm,
    spec_ref, base_ref, load_sem, save_sem,
):
    middle = base_ref.shape[2] // 2
    loads = [
        pltpu.make_async_copy(ref, base_ref.at[:, :, pl.ds(side * middle, middle), :], load_sem.at[side])
        for side, ref in enumerate((low_hbm, high_hbm))
    ]
    for load in loads:
        load.start()
    channels, half_y, _ = pooled_ref.shape
    local_x = base_ref.shape[1]
    modes = ty_ref.shape[1] // 3
    rows_per_mode = slab_ref.shape[0] // modes
    parts = tz_ref.shape[0] // (3 * 128)
    chunks = rows_per_mode // parts
    per_row = channels // chunks
    stacked = []
    for h in range(chunks):
        wide = jnp.concatenate(
            [slab_ref[pl.ds(p * chunks + h, modes, stride=rows_per_mode), :] for p in range(parts)], 1
        )
        stacked.append(dot_left3(ty_ref[...], wide))
    grown = jnp.concatenate(stacked, 0)
    high, low = split(grown)
    left = jnp.concatenate([high, low, high], 1)
    lane = lax.broadcasted_iota(jnp.int32, left.shape, 1) // (128 // per_row) % per_row

    for c in range(per_row):
        done = dot(jnp.where(lane == c, left, jnp.zeros_like(left)), tz_ref[...])
        for h in range(chunks):
            spec_ref[h * per_row + c] = done[h * half_y : (h + 1) * half_y]

    for load in loads:
        load.wait()
    saves = []
    for g in range(half_y // 16):
        at = [pl.ds(g * 16 + 8 * k, 8) for k in range(2)]
        pooled = jnp.concatenate([pooled_ref[:, a, :].reshape(channels * 8, 128) for a in at], 1)
        spectral = jnp.concatenate([spec_ref[:, a, :].reshape(channels * 8, 128) for a in at], 1)
        added = dot_left3(proj_ref[...], gelu(pooled + spectral))
        for k in range(2):
            for b in range(2):
                piece = added[b * channels * 8 : (b + 1) * channels * 8, k * 128 : (k + 1) * 128]
                piece = piece.reshape(channels, 8, 128)
                rows = pl.ds(g * 32 + 16 * k + 8 * b, 8)
                for x in range(local_x):
                    base_ref[:, x, rows, :] += piece
        rows = pl.ds(g * 32, 32)
        save = pltpu.make_async_copy(
            base_ref.at[:, :, rows, :], out_hbm.at[:, :, rows, :], save_sem.at[g]
        )
        save.start()
        saves.append(save)
    for save in saves:
        save.wait()


def on_device(features, fine_weights, middle_weights, lift_fine, lift_middle, project_out):
    channels, local_x, cells_y, cells_z = features.shape
    n = lax.axis_size("gx")
    owned = fine_weights.shape[0]
    owned_c = middle_weights.shape[0]
    half_ky, half_kz = KY // 2, KZ // 2
    narrow = 8
    fits = (
        owned == 3 * KZ
        and KZ == 32
        and KY == 3 * n
        and owned_c % narrow == 0
        and local_x == 2
        and cells_z == 128
        and cells_y % 32 == 0
        and channels % 16 == 0
    )
    if not fits:
        return general_device(
            features, fine_weights, middle_weights, lift_fine, lift_middle, project_out
        )
    modes_x = fine_weights.shape[1]
    modes_c = middle_weights.shape[1]
    tx = np.asarray(host_table(modes_x, local_x * n), np.float32).reshape(modes_x, n, local_x)
    txc = np.asarray(host_table(modes_c, n), np.float32)
    wire = forward_fine(features, KY, KZ, n)
    slab, lifted, liftm, proj, projm = mix_fine(
        wire, fine_weights, features, (lift_fine, lift_middle, project_out), tx, n
    )

    half_y, half_z = cells_y // 2, cells_z // 2
    pool_y = np.repeat(np.eye(half_y), 2, axis=1) * 0.5
    pool_z = np.repeat(np.eye(half_z), 2, axis=1) * 0.25
    ty_c = host_table(half_ky, half_y)
    tz_c = host_table(half_kz, half_z)
    parts = half_kz // narrow
    per_c = 128 // narrow
    chunks_c = channels // per_c
    yc = left_rows(np.concatenate([pool_y, ty_c @ pool_y], 0))
    zc_full = (tz_c @ pool_z).T.reshape(cells_z, parts, 1, narrow)
    zc = right_three(np.broadcast_to(zc_full, (cells_z, parts, per_c, narrow)).reshape(cells_z, -1))
    zp = np.repeat(pool_z, 2, axis=0).T
    zp = np.asarray(zp, jnp.bfloat16)
    zp = jnp.asarray(np.concatenate([zp, zp], 0))
    ty_i = left_three(host_table(KY, cells_y).T)
    tz_i = right_three(np.tile(host_table(KZ, cells_z), (4, 1)))
    level, pooled, coarse = pl.pallas_call(
        middle_kernel,
        out_shape=(
            jax.ShapeDtypeStruct(features.shape, F32),
            jax.ShapeDtypeStruct((channels, half_y, 128), F32),
            jax.ShapeDtypeStruct((half_ky * parts * chunks_c, 128), F32),
        ),
        in_specs=[whole(), far()] + [whole()] * 5,
        out_specs=(far(), whole(), whole()),
        scratch_shapes=[
            pltpu.VMEM(features.shape, F32),
            pltpu.VMEM((channels, cells_y, cells_z), F32),
            pltpu.VMEM((KY * local_x * channels, cells_z), F32),
            pltpu.VMEM(features.shape, F32),
            pltpu.SemaphoreType.DMA((2,)),
        ],
        name="middle",
    )(slab, lifted, ty_i, tz_i, yc, zc, zp)

    count = owned_c // narrow
    rows = count * chunks_c
    modal, base_low = coarse_call(
        coarse_out_kernel, n, txc, rows, 1, ((modes_c, rows, 128),),
        coarse, features, level, proj,
    )
    modal = modal.reshape(modes_c, count, channels, narrow).transpose(1, 3, 0, 2)
    mixed = mix_modes(modal.reshape(owned_c, modes_c, channels), middle_weights)
    mixed = mixed.reshape(count, narrow, modes_c, channels).transpose(2, 0, 3, 1)
    slab, base_high, lifted = coarse_call(
        coarse_back_kernel, n, txc, rows, 2, ((n * rows, 128), pooled.shape),
        mixed.reshape(modes_c, rows, 128), features, level, proj, pooled, liftm,
    )

    tyc_i = left_three(ty_c.T)
    grown = np.repeat(tz_c, 2, axis=1).reshape(parts, 1, narrow, cells_z)
    tzc_i = right_three(np.broadcast_to(grown, (parts, per_c, narrow, cells_z)).reshape(-1, cells_z))
    return pl.pallas_call(
        final_kernel,
        out_shape=jax.ShapeDtypeStruct(features.shape, F32),
        in_specs=[whole(), whole(), far(), far()] + [whole()] * 3,
        out_specs=far(),
        scratch_shapes=[
            pltpu.VMEM((channels, half_y, 128), F32),
            pltpu.VMEM(features.shape, F32),
            pltpu.SemaphoreType.DMA((2,)),
            pltpu.SemaphoreType.DMA((half_y // 16,)),
        ],
        name="final",
    )(slab, lifted, base_low, base_high, tyc_i, tzc_i, projm)


def solution(mesh):
    in_specs = (
        P(None, ("groups", "gx"), None, None),
        P("gx", None, None, None),
        P("gx", None, None, None),
        P(),
        P(),
        P(),
    )
    out_specs = P(None, ("groups", "gx"), None, None)
    return jax.shard_map(
        on_device, mesh=mesh, in_specs=in_specs, out_specs=out_specs, check_vma=False
    )
```

```python
import functools

import jax
import jax.numpy as jnp
import numpy as np
from jax import lax
from jax.experimental import pallas as pl
from jax.experimental.pallas import tpu as pltpu
from jax.sharding import PartitionSpec as P

KY = 48
KZ = 32


HIGHEST = lax.Precision.HIGHEST


def cosine_table(modes_kept, length, columns):
    orders = jnp.arange(modes_kept, dtype=jnp.int32)[:, None]
    points = jnp.arange(columns, dtype=jnp.int32)[None, :]
    phase = orders * (2 * points + 1) % (4 * length)
    angle = jnp.pi / (2 * length) * phase.astype(jnp.float32)
    scales = jnp.where(
        orders == 0, jnp.sqrt(jnp.float32(1.0 / length)), jnp.sqrt(jnp.float32(2.0 / length))
    )
    return scales * jnp.cos(angle)


def forward_yz(values, modes_y, modes_z):
    channels, local_x, cells_y, cells_z = values.shape
    table_z = cosine_table(modes_z, cells_z, cells_z)
    table_y = cosine_table(modes_y, cells_y, cells_y)
    along_z = jnp.einsum("cxyz,jz->cxyj", values, table_z, precision=HIGHEST)
    both = jnp.einsum("cxyj,iy->ijxc", along_z, table_y, precision=HIGHEST)
    return both.reshape(modes_y * modes_z, local_x, channels)


def inverse_yz(coeffs, modes_y, modes_z, cells_y, cells_z):
    total, local_x, channels = coeffs.shape
    shaped = coeffs.reshape(modes_y, modes_z, local_x, channels)
    table_z = cosine_table(modes_z, cells_z, cells_z)
    table_y = cosine_table(modes_y, cells_y, cells_y)
    along_y = jnp.einsum("ijxc,iy->jxcy", shaped, table_y, precision=HIGHEST)
    return jnp.einsum("jxcy,jz->cxyz", along_y, table_z, precision=HIGHEST)


def mix_modes(modal, weights):
    return jnp.einsum(
        "mkc,mkco->mko", modal.astype(jnp.bfloat16), weights, preferred_element_type=jnp.float32
    )


def pointwise(values, matrix):
    return jnp.einsum("cxyz,co->oxyz", values, matrix, precision=HIGHEST)


def coarsen(values):
    channels, cells_x, cells_y, cells_z = values.shape
    shaped = values.reshape(channels, cells_x // 2, 2, cells_y // 2, 2, cells_z // 2, 2)
    return jnp.mean(shaped, axis=(2, 4, 6))


def refine(values):
    return jnp.repeat(jnp.repeat(jnp.repeat(values, 2, axis=1), 2, axis=2), 2, axis=3)


def general_device(features, fine_weights, middle_weights, lift_fine, lift_middle, project_out):
    channels, local_x, cells_y, cells_z = features.shape
    group_size = lax.axis_size("gx")
    cells_x = local_x * group_size
    modes_x = fine_weights.shape[1]
    coeffs = forward_yz(features, KY, KZ)
    table_x = cosine_table(modes_x, cells_x, cells_x)
    owned_pairs = coeffs.shape[0] // group_size
    grouped = coeffs.reshape(group_size, owned_pairs, local_x, channels)
    modal = jnp.einsum(
        "amxc,kx->mkc",
        lax.all_to_all(grouped, "gx", split_axis=0, concat_axis=2, tiled=True),
        table_x,
        precision=HIGHEST,
    )
    mixed = mix_modes(modal, fine_weights)
    back = jnp.einsum("mkc,kx->mxc", mixed, table_x, precision=HIGHEST)
    slabs = lax.all_to_all(back, "gx", split_axis=1, concat_axis=0, tiled=True)
    level_one = jax.nn.gelu(
        inverse_yz(slabs, KY, KZ, cells_y, cells_z) + pointwise(features, lift_fine),
        approximate=False,
    )
    pooled = coarsen(level_one)
    half_x = local_x // 2
    half_ky = KY // 2
    half_kz = KZ // 2
    half_modes = middle_weights.shape[1]
    coarse_x = half_x * group_size
    coarse_coeffs = forward_yz(pooled, half_ky, half_kz)
    coarse_pencils = lax.all_to_all(coarse_coeffs, "gx", split_axis=0, concat_axis=1, tiled=True)
    coarse_table = cosine_table(half_modes, coarse_x, coarse_x)
    coarse_modal = jnp.einsum("mxc,kx->mkc", coarse_pencils, coarse_table, precision=HIGHEST)
    coarse_mixed = mix_modes(coarse_modal, middle_weights)
    coarse_back = jnp.einsum("mkc,kx->mxc", coarse_mixed, coarse_table, precision=HIGHEST)
    coarse_slabs = lax.all_to_all(coarse_back, "gx", split_axis=1, concat_axis=0, tiled=True)
    level_two = jax.nn.gelu(
        inverse_yz(coarse_slabs, half_ky, half_kz, cells_y // 2, cells_z // 2)
        + pointwise(pooled, lift_middle),
        approximate=False,
    )
    return features + pointwise(level_one + refine(level_two), project_out)


BF16 = jnp.bfloat16
MESH = pl.DeviceIdType.MESH
F32 = jnp.float32


def host_table(modes_kept, length):
    orders = np.arange(modes_kept)[:, None]
    points = np.arange(length)[None, :]
    scales = np.where(orders == 0, np.sqrt(1.0 / length), np.sqrt(2.0 / length))
    return scales * np.cos(np.pi * orders * (2 * points + 1) / (2 * length))


def host_split(table):
    table = np.asarray(table, np.float32)
    high = table.astype(jnp.bfloat16)
    low = (table - high.astype(np.float32)).astype(jnp.bfloat16)
    return high, low


def left_rows(table):
    high, low = host_split(table)
    return jnp.asarray(
        np.concatenate([np.concatenate([high, high], 1), np.concatenate([low, low], 1)], 0)
    )


def left_three(table):
    high, low = host_split(table)
    return jnp.asarray(np.concatenate([high, high, low], 1))


def right_three(table):
    high, low = host_split(table)
    return jnp.asarray(np.concatenate([high, high, low], 0))


def split(values):
    high = values.astype(BF16)
    low = (values - high.astype(F32)).astype(BF16)
    return high, low


def dot(left, right):
    return jnp.dot(left, right, preferred_element_type=F32)


def dot_left3(left3, values):
    high, low = split(values)
    return dot(left3, jnp.concatenate([high, low, high], 0))


def dot_right3(values, right3):
    high, low = split(values)
    return dot(jnp.concatenate([high, low, high], 1), right3)


def gelu(t):
    return 0.5 * t * (1.0 + lax.erf(t * np.float32(np.sqrt(0.5))))


def far():
    return pl.BlockSpec(memory_space=pl.ANY)


def whole():
    return pl.BlockSpec(memory_space=pltpu.VMEM)


def forward_kernel(f_ref, ty_ref, tz_ref, out_ref, grown_ref):
    step = pl.program_id(0)
    block, local_x, cells_y, cells_z = f_ref.shape
    modes = ty_ref.shape[0] // 2
    n = out_ref.shape[0]
    per = modes // n
    rows = grown_ref.shape[0] // modes
    channels = rows // local_x
    half = channels // 2
    for c in range(block):
        wide = jnp.concatenate([f_ref[c, x] for x in range(local_x)], 1)
        high, low = split(wide)
        both = dot(ty_ref[...], jnp.concatenate([high, low], 0))
        both = both[:modes] + both[modes:]
        for x in range(local_x):
            grown_ref[pl.ds(x * channels + step * block + c, modes, stride=rows), :] = both[
                :, x * cells_z : (x + 1) * cells_z
            ]

    @pl.when(step == pl.num_programs(0) - 1)
    def _():
        lane = lax.broadcasted_iota(jnp.int32, (3 * half, 128), 1) // 32

        def owner(a, carry):
            at = pl.multiple_of(a * per * rows, 8)
            done = dot_right3(grown_ref[pl.ds(at, per * rows), :], tz_ref[...])
            total = jnp.concatenate([done[g * rows + 3 * half : (g + 1) * rows] for g in range(per)], 0)
            for g in range(per):
                total = jnp.where(lane == g, done[g * rows : g * rows + 3 * half], total)
            out_ref[a] = total
            return carry

        lax.fori_loop(0, n, owner, 0, unroll=4)


def forward_fine(features, modes_y, modes_z, n):
    channels, local_x, cells_y, cells_z = features.shape
    block = 8
    ty = left_rows(host_table(modes_y, cells_y))
    tz = right_three(np.tile(host_table(modes_z, cells_z).T, (1, 4)))
    shape = (n, modes_y // n * channels // 2, 128)
    return pl.pallas_call(
        forward_kernel,
        grid=(channels // block,),
        out_shape=jax.ShapeDtypeStruct(shape, F32),
        in_specs=[
            pl.BlockSpec((block, local_x, cells_y, cells_z), lambda h: (h, 0, 0, 0)),
            pl.BlockSpec(ty.shape, lambda h: (0, 0)),
            pl.BlockSpec(tz.shape, lambda h: (0, 0)),
        ],
        out_specs=pl.BlockSpec(shape, lambda h: (0, 0, 0)),
        scratch_shapes=[pltpu.VMEM((modes_y * local_x * channels, cells_z), F32)],
        name="forward_fine",
    )(features, ty, tz)


def middle_kernel(
    slab_ref, f_hbm, ty_ref, tz_ref, yc_ref, zc_ref, zp_ref,
    level_hbm, pooled_ref, coarse_ref, spec_ref, sum_ref, grown_ref, f_ref, move_sem,
):
    load = pltpu.make_async_copy(f_hbm, f_ref, move_sem.at[0])
    load.start()
    save = pltpu.make_async_copy(f_ref, level_hbm, move_sem.at[1])
    channels, local_x, cells_y, cells_z = f_ref.shape
    modes_y = ty_ref.shape[1] // 3
    n = slab_ref.shape[0]
    per = modes_y // n
    half = channels // 2
    rows = 2 * channels
    lane = lax.broadcasted_iota(jnp.int32, (rows, 128), 1) // 32
    tail = lax.broadcasted_iota(jnp.int32, (rows, 128), 0) >= 3 * half

    def inverse(a, carry):
        lefts = []
        for g in range(per):
            value = jnp.concatenate([slab_ref[a], slab_ref[a, g * half : (g + 1) * half]], 0)
            lefts.append(jnp.where(lane == jnp.where(tail, 3, g), value, 0.0))
        done = dot_right3(jnp.concatenate(lefts, 0), tz_ref[...])
        grown_ref[pl.ds(pl.multiple_of(a * per * rows, 8), per * rows), :] = done
        return carry

    lax.fori_loop(0, n, inverse, 0, unroll=4)

    def inverse_y(o, carry):
        wide = jnp.concatenate(
            [grown_ref[pl.ds(x * channels + o, modes_y, stride=rows), :] for x in range(local_x)], 1
        )
        done = dot_left3(ty_ref[...], wide)
        for x in range(local_x):
            spec_ref[o, x] = done[:, x * cells_z : (x + 1) * cells_z]
        return carry

    lax.fori_loop(0, channels, inverse_y, 0, unroll=4)

    load.wait()

    def block(o, carry):
        level = [gelu(f_ref[o, x] + spec_ref[o, x]) for x in range(local_x)]
        for x in range(local_x):
            f_ref[o, x] = level[x]
        sum_ref[o] = level[0] + level[1]
        return carry

    lax.fori_loop(0, channels, block, 0, unroll=2)
    save.start()

    half_y = cells_y // 2
    modes_c = yc_ref.shape[0] // 2 - half_y
    parts = zc_ref.shape[1] // 128
    coarse_chunks = coarse_ref.shape[0] // (modes_c * parts)
    coarse_per = channels // coarse_chunks
    coarse_lane = (
        lax.broadcasted_iota(jnp.int32, (modes_c, parts * 128), 1) // (128 // coarse_per) % coarse_per
    )
    rows = modes_c + half_y

    def coarse(h, carry):
        total = jnp.zeros((modes_c, parts * 128), F32)
        for pair in range(coarse_per // 2):
            first = h * coarse_per + pair * 2
            wide = jnp.concatenate([sum_ref[first], sum_ref[first + 1]], 1)
            high, low = split(wide)
            both = dot(yc_ref[...], jnp.concatenate([high, low], 0))
            both = both[:rows] + both[rows:]
            modal = jnp.concatenate([both[half_y:, :128], both[half_y:, 128:]], 0)
            done = dot_right3(modal, zc_ref[...])
            for k in range(2):
                total = jnp.where(
                    coarse_lane == pair * 2 + k, done[k * modes_c : (k + 1) * modes_c], total
                )
            flat = jnp.concatenate([both[:half_y, :128], both[:half_y, 128:]], 0)
            high, low = split(flat)
            mean = dot(jnp.concatenate([high, low], 1), zp_ref[...])
            pooled_ref[first] = mean[:half_y]
            pooled_ref[first + 1] = mean[half_y:]
        for p in range(parts):
            coarse_ref[pl.ds(p * coarse_chunks + h, modes_c, stride=parts * coarse_chunks), :] = total[
                :, p * 128 : (p + 1) * 128
            ]
        return carry

    lax.fori_loop(0, coarse_chunks, coarse, 0)
    save.wait()


def widen(matrix_ref, targets):
    channels = matrix_ref.shape[0]
    size = channels * 8
    row = lax.broadcasted_iota(jnp.int32, (size, channels), 0) // 8
    pick = (row == lax.broadcasted_iota(jnp.int32, (size, channels), 1)).astype(F32).astype(BF16)
    col = lax.broadcasted_iota(jnp.int32, (channels, size), 1) // 8
    place = (col == lax.broadcasted_iota(jnp.int32, (channels, size), 0)).astype(F32).astype(BF16)
    left = lax.broadcasted_iota(jnp.int32, (size, size), 0) % 8
    right = lax.broadcasted_iota(jnp.int32, (size, size), 1) % 8
    for part, spots in zip(split(matrix_ref[...]), ((0, 1), (2,))):
        grown = lax.dot_general(pick, part, (((1,), (1,)), ((), ())), preferred_element_type=F32)
        grown = dot(grown.astype(BF16), place)
        for ref, at, rule in targets:
            value = jnp.where(rule(left, right), grown, 0.0).astype(BF16)
            for spot in spots:
                ref[at : at + size, spot * size : (spot + 1) * size] = value


def same(left, right):
    return left == right


def load_block(ref, at):
    channels, local_x, _, cells_z = ref.shape
    return jnp.concatenate([ref[:, x, at, :].reshape(channels * 8, cells_z) for x in range(local_x)], 1)


def store_block(ref, at, value):
    channels, local_x, _, cells_z = ref.shape
    for x in range(local_x):
        ref[:, x, at, :] = value[:, x * cells_z : (x + 1) * cells_z].reshape(channels, 8, cells_z)


def greet(n):
    me = lax.axis_index("gx")
    barrier = pltpu.get_barrier_semaphore()
    for d in range(1, n):
        pl.semaphore_signal(barrier, 1, device_id={"gx": lax.rem(me + d, n)}, device_id_type=MESH)
    pl.semaphore_wait(barrier, n - 1)


def swap(n, source, target, send_sem, recv_sem, own_sem, work):
    me = lax.axis_index("gx")
    copies = []
    for d in range(1, n):
        peer = lax.rem(me + d, n)
        copy = pltpu.make_async_remote_copy(
            src_ref=source.at[peer],
            dst_ref=target.at[me],
            send_sem=send_sem.at[d],
            recv_sem=recv_sem.at[d],
            device_id={"gx": peer},
            device_id_type=MESH,
        )
        copy.start()
        copies.append(copy)
    own = pltpu.make_async_copy(source.at[me], target.at[me], own_sem)
    own.start()
    work()
    for copy in copies:
        copy.wait()
    own.wait()


class Half:
    def __init__(self, side, f_hbm, level_hbm, wide_ref, base_hbm, f_ref, level_ref, sem):
        rows = f_ref.shape[2]
        at = pl.ds(side * rows, rows)
        self.loads = [
            pltpu.make_async_copy(f_hbm.at[:, :, at, :], f_ref, sem.at[0]),
            pltpu.make_async_copy(level_hbm.at[:, :, at, :], level_ref, sem.at[1]),
        ]
        self.save = pltpu.make_async_copy(f_ref, base_hbm, sem.at[2])
        self.refs = f_ref, level_ref, wide_ref

    def start(self):
        for load in self.loads:
            load.start()

    def work(self):
        f_ref, level_ref, wide_ref = self.refs
        for load in self.loads:
            load.wait()

        def block(b, carry):
            at = pl.ds(pl.multiple_of(b * 8, 8), 8)
            done = dot_left3(wide_ref[...], load_block(level_ref, at))
            store_block(f_ref, at, load_block(f_ref, at) + done)
            return carry

        lax.fori_loop(0, f_ref.shape[2] // 8, block, 0, unroll=2)
        self.save.start()


def coarse_out_kernel(
    n, tx, in_ref, f_hbm, level_hbm, wide_ref, out_ref, base_hbm,
    stage, got, send_sem, recv_sem, own_sem, f_ref, level_ref, move_sem,
):
    half = Half(0, f_hbm, level_hbm, wide_ref, base_hbm, f_ref, level_ref, move_sem)
    half.start()
    rows = stage.shape[1]
    for a in range(n):
        stage[a] = in_ref[a * rows : (a + 1) * rows]
    greet(n)
    swap(n, stage, got, send_sem, recv_sem, own_sem, half.work)
    for k in range(out_ref.shape[0]):
        out_ref[k] = sum(got[a] * np.float32(tx[k, a]) for a in range(n))
    half.save.wait()


def coarse_back_kernel(
    n, tx, in_ref, f_hbm, level_hbm, proj_ref, pooled_ref, wide_ref, out_ref, base_hbm, lifted_ref,
    stage, got, send_sem, recv_sem, own_sem, f_ref, level_ref, move_sem,
):
    half = Half(1, f_hbm, level_hbm, proj_ref, base_hbm, f_ref, level_ref, move_sem)
    half.start()
    rows = stage.shape[1]
    for a in range(n):
        stage[a] = sum(in_ref[k] * np.float32(tx[k, a]) for k in range(in_ref.shape[0]))
    greet(n)
    channels, half_y, _ = pooled_ref.shape

    def work():
        def block(g, carry):
            at = [pl.ds(pl.multiple_of(g * 16 + 8 * k, 8), 8) for k in range(2)]
            pooled = jnp.concatenate([pooled_ref[:, a, :].reshape(channels * 8, 128) for a in at], 1)
            done = dot_left3(wide_ref[...], pooled)
            for k in range(2):
                lifted_ref[:, at[k], :] = done[:, k * 128 : (k + 1) * 128].reshape(channels, 8, 128)
            return carry

        lax.fori_loop(0, half_y // 16, block, 0)
        half.work()

    swap(n, stage, got, send_sem, recv_sem, own_sem, work)
    for a in range(n):
        out_ref[a * rows : (a + 1) * rows] = got[a]
    half.save.wait()


def coarse_call(kernel, n, tx, rows, number, shapes, *values):
    channels, local_x, cells_y, cells_z = values[1].shape
    part = (channels, local_x, cells_y // 2, cells_z)
    shapes = (shapes[0], part) + tuple(shapes[1:])
    return pl.pallas_call(
        functools.partial(kernel, n, tx),
        out_shape=tuple(jax.ShapeDtypeStruct(shape, F32) for shape in shapes),
        in_specs=[whole(), far(), far()] + [whole()] * (len(values) - 3),
        out_specs=(whole(), far()) + (whole(),) * (len(shapes) - 2),
        scratch_shapes=[
            pltpu.VMEM((n, rows, 128), F32),
            pltpu.VMEM((n, rows, 128), F32),
            pltpu.SemaphoreType.DMA((n,)),
            pltpu.SemaphoreType.DMA((n,)),
            pltpu.SemaphoreType.DMA,
            pltpu.VMEM(part, F32),
            pltpu.VMEM(part, F32),
            pltpu.SemaphoreType.DMA((3,)),
        ],
        compiler_params=pltpu.CompilerParams(collective_id=number, has_side_effects=True),
        name=kernel.__name__,
    )(*values)


def mix_kernel(
    n, tx, wire_ref, w_hbm, f_hbm, lift_ref, middle_ref, project_ref,
    out_ref, lifted_hbm, middle_wide, proj_wide, final_wide, f_ref, move_sem, lift_wide, got, w_ref, modal, mixed, back,
    send_one, recv_one, send_two, recv_two, own_sem, w_sem,
):
    modes_x, channels, _, owned = w_ref.shape
    half = channels // 2
    fetch = pltpu.make_async_copy(w_hbm, w_ref, w_sem)
    fetch.start()
    load = pltpu.make_async_copy(f_hbm, f_ref, move_sem.at[0])
    load.start()
    save = pltpu.make_async_copy(f_ref, lifted_hbm, move_sem.at[1])
    greet(n)

    def lift():
        widen(lift_ref, ((lift_wide, 0, same),))
        load.wait()

        def block(b, carry):
            at = pl.ds(pl.multiple_of(b * 8, 8), 8)
            store_block(f_ref, at, dot_left3(lift_wide[...], load_block(f_ref, at)))
            return carry

        lax.fori_loop(0, f_ref.shape[2] // 8, block, 0)
        save.start()

    swap(n, wire_ref, got, send_one, recv_one, own_sem.at[0], lift)
    fetch.wait()
    lane = lax.broadcasted_iota(jnp.int32, (half, 128), 1)
    for k in range(modes_x):
        first = sum(got[a, :channels] * np.float32(tx[k, a, 0]) for a in range(n))
        second = sum(got[a] * np.float32(tx[k, a, 1]) for a in range(n))
        extra = jnp.zeros((half, 128), F32)
        for g in range(3):
            piece = pltpu.roll(second[g * half : (g + 1) * half], 32 * (g + 1), 1)
            extra = jnp.where(lane // 32 == g, piece, extra)
        total = first + jnp.concatenate([second[channels:], extra], 0)
        modal[k] = total.astype(BF16).astype(F32)
    mixed[...] = jnp.zeros_like(mixed)

    def mode(k, carry):
        total = jnp.zeros((channels, owned), F32)
        for c in range(channels):
            total += modal[k, c : c + 1, :owned] * w_ref[k, c].astype(F32)
        mixed[k, :, :owned] = total
        return carry

    lax.fori_loop(0, modes_x, mode, 0)
    wide = lax.broadcasted_iota(jnp.int32, (3 * half, 128), 1)
    for a in range(n):
        first = sum(mixed[k] * np.float32(tx[k, a, 0]) for k in range(modes_x))
        second = sum(mixed[k] * np.float32(tx[k, a, 1]) for k in range(modes_x))
        rolled = jnp.concatenate([pltpu.roll(second[half:], 96 - 32 * g, 1) for g in range(3)], 0)
        back[a] = jnp.where(wide < 96, jnp.concatenate([first, second[:half]], 0), rolled)

    def matrices():
        size = channels * 8
        widen(middle_ref, ((middle_wide, 0, same),))
        widen(
            project_ref,
            (
                (proj_wide, 0, same),
                (final_wide, 0, lambda left, right: left // 2 == right),
                (final_wide, size, lambda left, right: left // 2 + 4 == right),
            ),
        )

    swap(n, back, out_ref, send_two, recv_two, own_sem.at[1], matrices)
    save.wait()


def mix_fine(wire, weights, features, matrices, tx, n):
    turned = jnp.transpose(weights, (1, 2, 3, 0))
    modes_x, channels = turned.shape[:2]
    size = channels * 8
    wide = jax.ShapeDtypeStruct((size, 3 * size), BF16)
    return pl.pallas_call(
        functools.partial(mix_kernel, n, tx),
        out_shape=(
            jax.ShapeDtypeStruct(wire.shape, F32),
            jax.ShapeDtypeStruct(features.shape, F32),
            wide,
            wide,
            jax.ShapeDtypeStruct((2 * size, 3 * size), BF16),
        ),
        in_specs=[whole(), far(), far()] + [whole()] * 3,
        out_specs=(whole(), far()) + (whole(),) * 3,
        scratch_shapes=[
            pltpu.VMEM(features.shape, F32),
            pltpu.SemaphoreType.DMA((2,)),
            pltpu.VMEM(wide.shape, BF16),
            pltpu.VMEM(wire.shape, F32),
            pltpu.VMEM(turned.shape, BF16),
            pltpu.VMEM((modes_x, channels, 128), F32),
            pltpu.VMEM((modes_x, channels, 128), F32),
            pltpu.VMEM(wire.shape, F32),
        ]
        + [pltpu.SemaphoreType.DMA((n,))] * 4
        + [pltpu.SemaphoreType.DMA((2,)), pltpu.SemaphoreType.DMA],
        compiler_params=pltpu.CompilerParams(collective_id=0, has_side_effects=True),
        name="mix_fine",
    )(wire, turned, features, *matrices)


def final_kernel(
    slab_ref, pooled_ref, low_hbm, high_hbm, ty_ref, tz_ref, proj_ref, out_hbm,
    spec_ref, base_ref, load_sem, save_sem,
):
    middle = base_ref.shape[2] // 2
    loads = [
        pltpu.make_async_copy(ref, base_ref.at[:, :, pl.ds(side * middle, middle), :], load_sem.at[side])
        for side, ref in enumerate((low_hbm, high_hbm))
    ]
    for load in loads:
        load.start()
    channels, half_y, _ = pooled_ref.shape
    local_x = base_ref.shape[1]
    modes = ty_ref.shape[1] // 3
    rows_per_mode = slab_ref.shape[0] // modes
    parts = tz_ref.shape[0] // (3 * 128)
    chunks = rows_per_mode // parts
    per_row = channels // chunks
    stacked = []
    for h in range(chunks):
        wide = jnp.concatenate(
            [slab_ref[pl.ds(p * chunks + h, modes, stride=rows_per_mode), :] for p in range(parts)], 1
        )
        stacked.append(dot_left3(ty_ref[...], wide))
    grown = jnp.concatenate(stacked, 0)
    high, low = split(grown)
    left = jnp.concatenate([high, low, high], 1)
    lane = lax.broadcasted_iota(jnp.int32, left.shape, 1) // (128 // per_row) % per_row

    for c in range(per_row):
        done = dot(jnp.where(lane == c, left, jnp.zeros_like(left)), tz_ref[...])
        for h in range(chunks):
            spec_ref[h * per_row + c] = done[h * half_y : (h + 1) * half_y]

    for load in loads:
        load.wait()
    saves = []
    for g in range(half_y // 16):
        at = [pl.ds(g * 16 + 8 * k, 8) for k in range(2)]
        pooled = jnp.concatenate([pooled_ref[:, a, :].reshape(channels * 8, 128) for a in at], 1)
        spectral = jnp.concatenate([spec_ref[:, a, :].reshape(channels * 8, 128) for a in at], 1)
        added = dot_left3(proj_ref[...], gelu(pooled + spectral))
        for k in range(2):
            for b in range(2):
                piece = added[b * channels * 8 : (b + 1) * channels * 8, k * 128 : (k + 1) * 128]
                piece = piece.reshape(channels, 8, 128)
                rows = pl.ds(g * 32 + 16 * k + 8 * b, 8)
                for x in range(local_x):
                    base_ref[:, x, rows, :] += piece
        rows = pl.ds(g * 32, 32)
        save = pltpu.make_async_copy(
            base_ref.at[:, :, rows, :], out_hbm.at[:, :, rows, :], save_sem.at[g]
        )
        save.start()
        saves.append(save)
    for save in saves:
        save.wait()


def on_device(features, fine_weights, middle_weights, lift_fine, lift_middle, project_out):
    channels, local_x, cells_y, cells_z = features.shape
    n = lax.axis_size("gx")
    owned = fine_weights.shape[0]
    owned_c = middle_weights.shape[0]
    half_ky, half_kz = KY // 2, KZ // 2
    narrow = 8
    fits = (
        owned == 3 * KZ
        and KZ == 32
        and KY == 3 * n
        and owned_c % narrow == 0
        and local_x == 2
        and cells_z == 128
        and cells_y % 32 == 0
        and channels % 16 == 0
    )
    if not fits:
        return general_device(
            features, fine_weights, middle_weights, lift_fine, lift_middle, project_out
        )
    modes_x = fine_weights.shape[1]
    modes_c = middle_weights.shape[1]
    tx = np.asarray(host_table(modes_x, local_x * n), np.float32).reshape(modes_x, n, local_x)
    txc = np.asarray(host_table(modes_c, n), np.float32)
    wire = forward_fine(features, KY, KZ, n)
    slab, lifted, liftm, proj, projm = mix_fine(
        wire, fine_weights, features, (lift_fine, lift_middle, project_out), tx, n
    )

    half_y, half_z = cells_y // 2, cells_z // 2
    pool_y = np.repeat(np.eye(half_y), 2, axis=1) * 0.5
    pool_z = np.repeat(np.eye(half_z), 2, axis=1) * 0.25
    ty_c = host_table(half_ky, half_y)
    tz_c = host_table(half_kz, half_z)
    parts = half_kz // narrow
    per_c = 128 // narrow
    chunks_c = channels // per_c
    yc = left_rows(np.concatenate([pool_y, ty_c @ pool_y], 0))
    zc_full = (tz_c @ pool_z).T.reshape(cells_z, parts, 1, narrow)
    zc = right_three(np.broadcast_to(zc_full, (cells_z, parts, per_c, narrow)).reshape(cells_z, -1))
    zp = np.repeat(pool_z, 2, axis=0).T
    zp = np.asarray(zp, jnp.bfloat16)
    zp = jnp.asarray(np.concatenate([zp, zp], 0))
    ty_i = left_three(host_table(KY, cells_y).T)
    tz_i = right_three(np.tile(host_table(KZ, cells_z), (4, 1)))
    level, pooled, coarse = pl.pallas_call(
        middle_kernel,
        out_shape=(
            jax.ShapeDtypeStruct(features.shape, F32),
            jax.ShapeDtypeStruct((channels, half_y, 128), F32),
            jax.ShapeDtypeStruct((half_ky * parts * chunks_c, 128), F32),
        ),
        in_specs=[whole(), far()] + [whole()] * 5,
        out_specs=(far(), whole(), whole()),
        scratch_shapes=[
            pltpu.VMEM(features.shape, F32),
            pltpu.VMEM((channels, cells_y, cells_z), F32),
            pltpu.VMEM((KY * local_x * channels, cells_z), F32),
            pltpu.VMEM(features.shape, F32),
            pltpu.SemaphoreType.DMA((2,)),
        ],
        name="middle",
    )(slab, lifted, ty_i, tz_i, yc, zc, zp)

    count = owned_c // narrow
    rows = count * chunks_c
    modal, base_low = coarse_call(
        coarse_out_kernel, n, txc, rows, 1, ((modes_c, rows, 128),),
        coarse, features, level, proj,
    )
    modal = modal.reshape(modes_c, count, channels, narrow).transpose(1, 3, 0, 2)
    mixed = mix_modes(modal.reshape(owned_c, modes_c, channels), middle_weights)
    mixed = mixed.reshape(count, narrow, modes_c, channels).transpose(2, 0, 3, 1)
    slab, base_high, lifted = coarse_call(
        coarse_back_kernel, n, txc, rows, 2, ((n * rows, 128), pooled.shape),
        mixed.reshape(modes_c, rows, 128), features, level, proj, pooled, liftm,
    )

    tyc_i = left_three(ty_c.T)
    grown = np.repeat(tz_c, 2, axis=1).reshape(parts, 1, narrow, cells_z)
    tzc_i = right_three(np.broadcast_to(grown, (parts, per_c, narrow, cells_z)).reshape(-1, cells_z))
    return pl.pallas_call(
        final_kernel,
        out_shape=jax.ShapeDtypeStruct(features.shape, F32),
        in_specs=[whole(), whole(), far(), far()] + [whole()] * 3,
        out_specs=far(),
        scratch_shapes=[
            pltpu.VMEM((channels, half_y, 128), F32),
            pltpu.VMEM(features.shape, F32),
            pltpu.SemaphoreType.DMA((2,)),
            pltpu.SemaphoreType.DMA((half_y // 16,)),
        ],
        name="final",
    )(slab, lifted, base_low, base_high, tyc_i, tzc_i, projm)


def solution(mesh):
    in_specs = (
        P(None, ("groups", "gx"), None, None),
        P("gx", None, None, None),
        P("gx", None, None, None),
        P(),
        P(),
        P(),
    )
    out_specs = P(None, ("groups", "gx"), None, None)
    return jax.shard_map(
        on_device, mesh=mesh, in_specs=in_specs, out_specs=out_specs, check_vma=False
    )
```

```python
import functools

import jax
import jax.numpy as jnp
import numpy as np
from jax import lax
from jax.experimental import pallas as pl
from jax.experimental.pallas import tpu as pltpu
from jax.sharding import PartitionSpec as P

KY = 48
KZ = 32


HIGHEST = lax.Precision.HIGHEST


def cosine_table(modes_kept, length, columns):
    orders = jnp.arange(modes_kept, dtype=jnp.int32)[:, None]
    points = jnp.arange(columns, dtype=jnp.int32)[None, :]
    phase = orders * (2 * points + 1) % (4 * length)
    angle = jnp.pi / (2 * length) * phase.astype(jnp.float32)
    scales = jnp.where(
        orders == 0, jnp.sqrt(jnp.float32(1.0 / length)), jnp.sqrt(jnp.float32(2.0 / length))
    )
    return scales * jnp.cos(angle)


def forward_yz(values, modes_y, modes_z):
    channels, local_x, cells_y, cells_z = values.shape
    table_z = cosine_table(modes_z, cells_z, cells_z)
    table_y = cosine_table(modes_y, cells_y, cells_y)
    along_z = jnp.einsum("cxyz,jz->cxyj", values, table_z, precision=HIGHEST)
    both = jnp.einsum("cxyj,iy->ijxc", along_z, table_y, precision=HIGHEST)
    return both.reshape(modes_y * modes_z, local_x, channels)


def inverse_yz(coeffs, modes_y, modes_z, cells_y, cells_z):
    total, local_x, channels = coeffs.shape
    shaped = coeffs.reshape(modes_y, modes_z, local_x, channels)
    table_z = cosine_table(modes_z, cells_z, cells_z)
    table_y = cosine_table(modes_y, cells_y, cells_y)
    along_y = jnp.einsum("ijxc,iy->jxcy", shaped, table_y, precision=HIGHEST)
    return jnp.einsum("jxcy,jz->cxyz", along_y, table_z, precision=HIGHEST)


def mix_modes(modal, weights):
    return jnp.einsum(
        "mkc,mkco->mko", modal.astype(jnp.bfloat16), weights, preferred_element_type=jnp.float32
    )


def pointwise(values, matrix):
    return jnp.einsum("cxyz,co->oxyz", values, matrix, precision=HIGHEST)


def coarsen(values):
    channels, cells_x, cells_y, cells_z = values.shape
    shaped = values.reshape(channels, cells_x // 2, 2, cells_y // 2, 2, cells_z // 2, 2)
    return jnp.mean(shaped, axis=(2, 4, 6))


def refine(values):
    return jnp.repeat(jnp.repeat(jnp.repeat(values, 2, axis=1), 2, axis=2), 2, axis=3)


def general_device(features, fine_weights, middle_weights, lift_fine, lift_middle, project_out):
    channels, local_x, cells_y, cells_z = features.shape
    group_size = lax.axis_size("gx")
    cells_x = local_x * group_size
    modes_x = fine_weights.shape[1]
    coeffs = forward_yz(features, KY, KZ)
    table_x = cosine_table(modes_x, cells_x, cells_x)
    owned_pairs = coeffs.shape[0] // group_size
    grouped = coeffs.reshape(group_size, owned_pairs, local_x, channels)
    modal = jnp.einsum(
        "amxc,kx->mkc",
        lax.all_to_all(grouped, "gx", split_axis=0, concat_axis=2, tiled=True),
        table_x,
        precision=HIGHEST,
    )
    mixed = mix_modes(modal, fine_weights)
    back = jnp.einsum("mkc,kx->mxc", mixed, table_x, precision=HIGHEST)
    slabs = lax.all_to_all(back, "gx", split_axis=1, concat_axis=0, tiled=True)
    level_one = jax.nn.gelu(
        inverse_yz(slabs, KY, KZ, cells_y, cells_z) + pointwise(features, lift_fine),
        approximate=False,
    )
    pooled = coarsen(level_one)
    half_x = local_x // 2
    half_ky = KY // 2
    half_kz = KZ // 2
    half_modes = middle_weights.shape[1]
    coarse_x = half_x * group_size
    coarse_coeffs = forward_yz(pooled, half_ky, half_kz)
    coarse_pencils = lax.all_to_all(coarse_coeffs, "gx", split_axis=0, concat_axis=1, tiled=True)
    coarse_table = cosine_table(half_modes, coarse_x, coarse_x)
    coarse_modal = jnp.einsum("mxc,kx->mkc", coarse_pencils, coarse_table, precision=HIGHEST)
    coarse_mixed = mix_modes(coarse_modal, middle_weights)
    coarse_back = jnp.einsum("mkc,kx->mxc", coarse_mixed, coarse_table, precision=HIGHEST)
    coarse_slabs = lax.all_to_all(coarse_back, "gx", split_axis=1, concat_axis=0, tiled=True)
    level_two = jax.nn.gelu(
        inverse_yz(coarse_slabs, half_ky, half_kz, cells_y // 2, cells_z // 2)
        + pointwise(pooled, lift_middle),
        approximate=False,
    )
    return features + pointwise(level_one + refine(level_two), project_out)


BF16 = jnp.bfloat16
MESH = pl.DeviceIdType.MESH
F32 = jnp.float32


def host_table(modes_kept, length):
    orders = np.arange(modes_kept)[:, None]
    points = np.arange(length)[None, :]
    scales = np.where(orders == 0, np.sqrt(1.0 / length), np.sqrt(2.0 / length))
    return scales * np.cos(np.pi * orders * (2 * points + 1) / (2 * length))


def host_split(table):
    table = np.asarray(table, np.float32)
    high = table.astype(jnp.bfloat16)
    low = (table - high.astype(np.float32)).astype(jnp.bfloat16)
    return high, low


def left_rows(table):
    high, low = host_split(table)
    return jnp.asarray(
        np.concatenate([np.concatenate([high, high], 1), np.concatenate([low, low], 1)], 0)
    )


def left_three(table):
    high, low = host_split(table)
    return jnp.asarray(np.concatenate([high, high, low], 1))


def right_three(table):
    high, low = host_split(table)
    return jnp.asarray(np.concatenate([high, high, low], 0))


def split(values):
    high = values.astype(BF16)
    low = (values - high.astype(F32)).astype(BF16)
    return high, low


def dot(left, right):
    return jnp.dot(left, right, preferred_element_type=F32)


def dot_left3(left3, values):
    high, low = split(values)
    return dot(left3, jnp.concatenate([high, low, high], 0))


def dot_right3(values, right3):
    high, low = split(values)
    return dot(jnp.concatenate([high, low, high], 1), right3)


def gelu(t):
    return 0.5 * t * (1.0 + lax.erf(t * np.float32(np.sqrt(0.5))))


def far():
    return pl.BlockSpec(memory_space=pl.ANY)


def whole():
    return pl.BlockSpec(memory_space=pltpu.VMEM)


def forward_kernel(f_ref, ty_ref, tz_ref, out_ref, grown_ref):
    step = pl.program_id(0)
    block, local_x, cells_y, cells_z = f_ref.shape
    modes = ty_ref.shape[0] // 2
    n = out_ref.shape[0]
    per = modes // n
    rows = grown_ref.shape[0] // modes
    channels = rows // local_x
    half = channels // 2
    for c in range(block):
        wide = jnp.concatenate([f_ref[c, x] for x in range(local_x)], 1)
        high, low = split(wide)
        both = dot(ty_ref[...], jnp.concatenate([high, low], 0))
        both = both[:modes] + both[modes:]
        for x in range(local_x):
            grown_ref[pl.ds(x * channels + step * block + c, modes, stride=rows), :] = both[
                :, x * cells_z : (x + 1) * cells_z
            ]

    @pl.when(step == pl.num_programs(0) - 1)
    def _():
        lane = lax.broadcasted_iota(jnp.int32, (3 * half, 128), 1) // 32

        def owner(a, carry):
            at = pl.multiple_of(a * per * rows, 8)
            done = dot_right3(grown_ref[pl.ds(at, per * rows), :], tz_ref[...])
            total = jnp.concatenate([done[g * rows + 3 * half : (g + 1) * rows] for g in range(per)], 0)
            for g in range(per):
                total = jnp.where(lane == g, done[g * rows : g * rows + 3 * half], total)
            out_ref[a] = total
            return carry

        lax.fori_loop(0, n, owner, 0, unroll=8)


def forward_fine(features, modes_y, modes_z, n):
    channels, local_x, cells_y, cells_z = features.shape
    block = 8
    ty = left_rows(host_table(modes_y, cells_y))
    tz = right_three(np.tile(host_table(modes_z, cells_z).T, (1, 4)))
    shape = (n, modes_y // n * channels // 2, 128)
    return pl.pallas_call(
        forward_kernel,
        grid=(channels // block,),
        out_shape=jax.ShapeDtypeStruct(shape, F32),
        in_specs=[
            pl.BlockSpec((block, local_x, cells_y, cells_z), lambda h: (h, 0, 0, 0)),
            pl.BlockSpec(ty.shape, lambda h: (0, 0)),
            pl.BlockSpec(tz.shape, lambda h: (0, 0)),
        ],
        out_specs=pl.BlockSpec(shape, lambda h: (0, 0, 0)),
        scratch_shapes=[pltpu.VMEM((modes_y * local_x * channels, cells_z), F32)],
        name="forward_fine",
    )(features, ty, tz)


def middle_kernel(
    slab_ref, f_hbm, ty_ref, tz_ref, yc_ref, zc_ref, zp_ref,
    level_hbm, pooled_ref, coarse_ref, spec_ref, sum_ref, grown_ref, f_ref, move_sem,
):
    load = pltpu.make_async_copy(f_hbm, f_ref, move_sem.at[0])
    load.start()
    save = pltpu.make_async_copy(f_ref, level_hbm, move_sem.at[1])
    channels, local_x, cells_y, cells_z = f_ref.shape
    modes_y = ty_ref.shape[1] // 3
    n = slab_ref.shape[0]
    per = modes_y // n
    half = channels // 2
    rows = 2 * channels
    lane = lax.broadcasted_iota(jnp.int32, (rows, 128), 1) // 32
    tail = lax.broadcasted_iota(jnp.int32, (rows, 128), 0) >= 3 * half

    def inverse(a, carry):
        lefts = []
        for g in range(per):
            value = jnp.concatenate([slab_ref[a], slab_ref[a, g * half : (g + 1) * half]], 0)
            lefts.append(jnp.where(lane == jnp.where(tail, 3, g), value, 0.0))
        done = dot_right3(jnp.concatenate(lefts, 0), tz_ref[...])
        grown_ref[pl.ds(pl.multiple_of(a * per * rows, 8), per * rows), :] = done
        return carry

    lax.fori_loop(0, n, inverse, 0, unroll=8)

    def inverse_y(o, carry):
        wide = jnp.concatenate(
            [grown_ref[pl.ds(x * channels + o, modes_y, stride=rows), :] for x in range(local_x)], 1
        )
        done = dot_left3(ty_ref[...], wide)
        for x in range(local_x):
            spec_ref[o, x] = done[:, x * cells_z : (x + 1) * cells_z]
        return carry

    lax.fori_loop(0, channels, inverse_y, 0, unroll=8)

    load.wait()

    def block(o, carry):
        level = [gelu(f_ref[o, x] + spec_ref[o, x]) for x in range(local_x)]
        for x in range(local_x):
            f_ref[o, x] = level[x]
        sum_ref[o] = level[0] + level[1]
        return carry

    lax.fori_loop(0, channels, block, 0, unroll=2)
    save.start()

    half_y = cells_y // 2
    modes_c = yc_ref.shape[0] // 2 - half_y
    parts = zc_ref.shape[1] // 128
    coarse_chunks = coarse_ref.shape[0] // (modes_c * parts)
    coarse_per = channels // coarse_chunks
    coarse_lane = (
        lax.broadcasted_iota(jnp.int32, (modes_c, parts * 128), 1) // (128 // coarse_per) % coarse_per
    )
    rows = modes_c + half_y

    def coarse(h, carry):
        total = jnp.zeros((modes_c, parts * 128), F32)
        for pair in range(coarse_per // 2):
            first = h * coarse_per + pair * 2
            wide = jnp.concatenate([sum_ref[first], sum_ref[first + 1]], 1)
            high, low = split(wide)
            both = dot(yc_ref[...], jnp.concatenate([high, low], 0))
            both = both[:rows] + both[rows:]
            modal = jnp.concatenate([both[half_y:, :128], both[half_y:, 128:]], 0)
            done = dot_right3(modal, zc_ref[...])
            for k in range(2):
                total = jnp.where(
                    coarse_lane == pair * 2 + k, done[k * modes_c : (k + 1) * modes_c], total
                )
            flat = jnp.concatenate([both[:half_y, :128], both[:half_y, 128:]], 0)
            high, low = split(flat)
            mean = dot(jnp.concatenate([high, low], 1), zp_ref[...])
            pooled_ref[first] = mean[:half_y]
            pooled_ref[first + 1] = mean[half_y:]
        for p in range(parts):
            coarse_ref[pl.ds(p * coarse_chunks + h, modes_c, stride=parts * coarse_chunks), :] = total[
                :, p * 128 : (p + 1) * 128
            ]
        return carry

    lax.fori_loop(0, coarse_chunks, coarse, 0, unroll=True)
    save.wait()


def widen(matrix_ref, targets):
    channels = matrix_ref.shape[0]
    size = channels * 8
    row = lax.broadcasted_iota(jnp.int32, (size, channels), 0) // 8
    pick = (row == lax.broadcasted_iota(jnp.int32, (size, channels), 1)).astype(F32).astype(BF16)
    col = lax.broadcasted_iota(jnp.int32, (channels, size), 1) // 8
    place = (col == lax.broadcasted_iota(jnp.int32, (channels, size), 0)).astype(F32).astype(BF16)
    left = lax.broadcasted_iota(jnp.int32, (size, size), 0) % 8
    right = lax.broadcasted_iota(jnp.int32, (size, size), 1) % 8
    for part, spots in zip(split(matrix_ref[...]), ((0, 1), (2,))):
        grown = lax.dot_general(pick, part, (((1,), (1,)), ((), ())), preferred_element_type=F32)
        grown = dot(grown.astype(BF16), place)
        for ref, at, rule in targets:
            value = jnp.where(rule(left, right), grown, 0.0).astype(BF16)
            for spot in spots:
                ref[at : at + size, spot * size : (spot + 1) * size] = value


def same(left, right):
    return left == right


def load_block(ref, at):
    channels, local_x, _, cells_z = ref.shape
    return jnp.concatenate([ref[:, x, at, :].reshape(channels * 8, cells_z) for x in range(local_x)], 1)


def store_block(ref, at, value):
    channels, local_x, _, cells_z = ref.shape
    for x in range(local_x):
        ref[:, x, at, :] = value[:, x * cells_z : (x + 1) * cells_z].reshape(channels, 8, cells_z)


def greet(n):
    me = lax.axis_index("gx")
    barrier = pltpu.get_barrier_semaphore()
    for d in range(1, n):
        pl.semaphore_signal(barrier, 1, device_id={"gx": lax.rem(me + d, n)}, device_id_type=MESH)
    pl.semaphore_wait(barrier, n - 1)


def swap(n, source, target, send_sem, recv_sem, own_sem, work):
    me = lax.axis_index("gx")
    copies = []
    for d in range(1, n):
        peer = lax.rem(me + d, n)
        copy = pltpu.make_async_remote_copy(
            src_ref=source.at[peer],
            dst_ref=target.at[me],
            send_sem=send_sem.at[d],
            recv_sem=recv_sem.at[d],
            device_id={"gx": peer},
            device_id_type=MESH,
        )
        copy.start()
        copies.append(copy)
    own = pltpu.make_async_copy(source.at[me], target.at[me], own_sem)
    own.start()
    work()
    for copy in copies:
        copy.wait()
    own.wait()


class Half:
    def __init__(self, side, f_hbm, level_hbm, wide_ref, base_hbm, f_ref, level_ref, sem):
        rows = f_ref.shape[2]
        at = pl.ds(side * rows, rows)
        self.loads = [
            pltpu.make_async_copy(f_hbm.at[:, :, at, :], f_ref, sem.at[0]),
            pltpu.make_async_copy(level_hbm.at[:, :, at, :], level_ref, sem.at[1]),
        ]
        self.save = pltpu.make_async_copy(f_ref, base_hbm, sem.at[2])
        self.refs = f_ref, level_ref, wide_ref

    def start(self):
        for load in self.loads:
            load.start()

    def work(self):
        f_ref, level_ref, wide_ref = self.refs
        for load in self.loads:
            load.wait()

        def block(b, carry):
            at = pl.ds(pl.multiple_of(b * 8, 8), 8)
            done = dot_left3(wide_ref[...], load_block(level_ref, at))
            store_block(f_ref, at, load_block(f_ref, at) + done)
            return carry

        lax.fori_loop(0, f_ref.shape[2] // 8, block, 0, unroll=3)
        self.save.start()


def coarse_out_kernel(
    n, tx, in_ref, f_hbm, level_hbm, wide_ref, out_ref, base_hbm,
    stage, got, send_sem, recv_sem, own_sem, f_ref, level_ref, move_sem,
):
    half = Half(0, f_hbm, level_hbm, wide_ref, base_hbm, f_ref, level_ref, move_sem)
    half.start()
    rows = stage.shape[1]
    for a in range(n):
        stage[a] = in_ref[a * rows : (a + 1) * rows]
    greet(n)
    swap(n, stage, got, send_sem, recv_sem, own_sem, half.work)
    for k in range(out_ref.shape[0]):
        out_ref[k] = sum(got[a] * np.float32(tx[k, a]) for a in range(n))
    half.save.wait()


def coarse_back_kernel(
    n, tx, in_ref, f_hbm, level_hbm, proj_ref, pooled_ref, wide_ref, out_ref, base_hbm, lifted_ref,
    stage, got, send_sem, recv_sem, own_sem, f_ref, level_ref, move_sem,
):
    half = Half(1, f_hbm, level_hbm, proj_ref, base_hbm, f_ref, level_ref, move_sem)
    half.start()
    rows = stage.shape[1]
    for a in range(n):
        stage[a] = sum(in_ref[k] * np.float32(tx[k, a]) for k in range(in_ref.shape[0]))
    greet(n)
    channels, half_y, _ = pooled_ref.shape

    def work():
        def block(g, carry):
            at = [pl.ds(pl.multiple_of(g * 16 + 8 * k, 8), 8) for k in range(2)]
            pooled = jnp.concatenate([pooled_ref[:, a, :].reshape(channels * 8, 128) for a in at], 1)
            done = dot_left3(wide_ref[...], pooled)
            for k in range(2):
                lifted_ref[:, at[k], :] = done[:, k * 128 : (k + 1) * 128].reshape(channels, 8, 128)
            return carry

        lax.fori_loop(0, half_y // 16, block, 0)
        half.work()

    swap(n, stage, got, send_sem, recv_sem, own_sem, work)
    for a in range(n):
        out_ref[a * rows : (a + 1) * rows] = got[a]
    half.save.wait()


def coarse_call(kernel, n, tx, rows, number, shapes, *values):
    channels, local_x, cells_y, cells_z = values[1].shape
    part = (channels, local_x, cells_y // 2, cells_z)
    shapes = (shapes[0], part) + tuple(shapes[1:])
    return pl.pallas_call(
        functools.partial(kernel, n, tx),
        out_shape=tuple(jax.ShapeDtypeStruct(shape, F32) for shape in shapes),
        in_specs=[whole(), far(), far()] + [whole()] * (len(values) - 3),
        out_specs=(whole(), far()) + (whole(),) * (len(shapes) - 2),
        scratch_shapes=[
            pltpu.VMEM((n, rows, 128), F32),
            pltpu.VMEM((n, rows, 128), F32),
            pltpu.SemaphoreType.DMA((n,)),
            pltpu.SemaphoreType.DMA((n,)),
            pltpu.SemaphoreType.DMA,
            pltpu.VMEM(part, F32),
            pltpu.VMEM(part, F32),
            pltpu.SemaphoreType.DMA((3,)),
        ],
        compiler_params=pltpu.CompilerParams(collective_id=number, has_side_effects=True),
        name=kernel.__name__,
    )(*values)


def mix_kernel(
    n, tx, wire_ref, w_hbm, f_hbm, lift_ref, middle_ref, project_ref,
    out_ref, lifted_hbm, middle_wide, proj_wide, final_wide, f_ref, move_sem, lift_wide, got, w_ref, modal, mixed, back,
    send_one, recv_one, send_two, recv_two, own_sem, w_sem,
):
    modes_x, channels, _, owned = w_ref.shape
    half = channels // 2
    fetch = pltpu.make_async_copy(w_hbm, w_ref, w_sem)
    fetch.start()
    load = pltpu.make_async_copy(f_hbm, f_ref, move_sem.at[0])
    load.start()
    save = pltpu.make_async_copy(f_ref, lifted_hbm, move_sem.at[1])
    greet(n)

    def lift():
        widen(lift_ref, ((lift_wide, 0, same),))
        load.wait()

        def block(b, carry):
            at = pl.ds(pl.multiple_of(b * 8, 8), 8)
            store_block(f_ref, at, dot_left3(lift_wide[...], load_block(f_ref, at)))
            return carry

        lax.fori_loop(0, f_ref.shape[2] // 8, block, 0)
        save.start()

    swap(n, wire_ref, got, send_one, recv_one, own_sem.at[0], lift)
    fetch.wait()
    lane = lax.broadcasted_iota(jnp.int32, (half, 128), 1)
    for k in range(modes_x):
        first = sum(got[a, :channels] * np.float32(tx[k, a, 0]) for a in range(n))
        second = sum(got[a] * np.float32(tx[k, a, 1]) for a in range(n))
        extra = jnp.zeros((half, 128), F32)
        for g in range(3):
            piece = pltpu.roll(second[g * half : (g + 1) * half], 32 * (g + 1), 1)
            extra = jnp.where(lane // 32 == g, piece, extra)
        total = first + jnp.concatenate([second[channels:], extra], 0)
        modal[k] = total.astype(BF16).astype(F32)
    mixed[...] = jnp.zeros_like(mixed)

    def mode(k, carry):
        total = jnp.zeros((channels, owned), F32)
        for c in range(channels):
            total += modal[k, c : c + 1, :owned] * w_ref[k, c].astype(F32)
        mixed[k, :, :owned] = total
        return carry

    lax.fori_loop(0, modes_x, mode, 0, unroll=2)
    wide = lax.broadcasted_iota(jnp.int32, (3 * half, 128), 1)
    for a in range(n):
        first = sum(mixed[k] * np.float32(tx[k, a, 0]) for k in range(modes_x))
        second = sum(mixed[k] * np.float32(tx[k, a, 1]) for k in range(modes_x))
        rolled = jnp.concatenate([pltpu.roll(second[half:], 96 - 32 * g, 1) for g in range(3)], 0)
        back[a] = jnp.where(wide < 96, jnp.concatenate([first, second[:half]], 0), rolled)

    def matrices():
        size = channels * 8
        widen(middle_ref, ((middle_wide, 0, same),))
        widen(
            project_ref,
            (
                (proj_wide, 0, same),
                (final_wide, 0, lambda left, right: left // 2 == right),
                (final_wide, size, lambda left, right: left // 2 + 4 == right),
            ),
        )

    swap(n, back, out_ref, send_two, recv_two, own_sem.at[1], matrices)
    save.wait()


def mix_fine(wire, weights, features, matrices, tx, n):
    turned = jnp.transpose(weights, (1, 2, 3, 0))
    modes_x, channels = turned.shape[:2]
    size = channels * 8
    wide = jax.ShapeDtypeStruct((size, 3 * size), BF16)
    return pl.pallas_call(
        functools.partial(mix_kernel, n, tx),
        out_shape=(
            jax.ShapeDtypeStruct(wire.shape, F32),
            jax.ShapeDtypeStruct(features.shape, F32),
            wide,
            wide,
            jax.ShapeDtypeStruct((2 * size, 3 * size), BF16),
        ),
        in_specs=[whole(), far(), far()] + [whole()] * 3,
        out_specs=(whole(), far()) + (whole(),) * 3,
        scratch_shapes=[
            pltpu.VMEM(features.shape, F32),
            pltpu.SemaphoreType.DMA((2,)),
            pltpu.VMEM(wide.shape, BF16),
            pltpu.VMEM(wire.shape, F32),
            pltpu.VMEM(turned.shape, BF16),
            pltpu.VMEM((modes_x, channels, 128), F32),
            pltpu.VMEM((modes_x, channels, 128), F32),
            pltpu.VMEM(wire.shape, F32),
        ]
        + [pltpu.SemaphoreType.DMA((n,))] * 4
        + [pltpu.SemaphoreType.DMA((2,)), pltpu.SemaphoreType.DMA],
        compiler_params=pltpu.CompilerParams(collective_id=0, has_side_effects=True),
        name="mix_fine",
    )(wire, turned, features, *matrices)


def final_kernel(
    slab_ref, pooled_ref, low_hbm, high_hbm, ty_ref, tz_ref, proj_ref, out_hbm,
    spec_ref, base_ref, load_sem, save_sem,
):
    middle = base_ref.shape[2] // 2
    loads = [
        pltpu.make_async_copy(ref, base_ref.at[:, :, pl.ds(side * middle, middle), :], load_sem.at[side])
        for side, ref in enumerate((low_hbm, high_hbm))
    ]
    for load in loads:
        load.start()
    channels, half_y, _ = pooled_ref.shape
    local_x = base_ref.shape[1]
    modes = ty_ref.shape[1] // 3
    rows_per_mode = slab_ref.shape[0] // modes
    parts = tz_ref.shape[0] // (3 * 128)
    chunks = rows_per_mode // parts
    per_row = channels // chunks
    stacked = []
    for h in range(chunks):
        wide = jnp.concatenate(
            [slab_ref[pl.ds(p * chunks + h, modes, stride=rows_per_mode), :] for p in range(parts)], 1
        )
        stacked.append(dot_left3(ty_ref[...], wide))
    grown = jnp.concatenate(stacked, 0)
    high, low = split(grown)
    left = jnp.concatenate([high, low, high], 1)
    lane = lax.broadcasted_iota(jnp.int32, left.shape, 1) // (128 // per_row) % per_row

    for c in range(per_row):
        done = dot(jnp.where(lane == c, left, jnp.zeros_like(left)), tz_ref[...])
        for h in range(chunks):
            spec_ref[h * per_row + c] = done[h * half_y : (h + 1) * half_y]

    for load in loads:
        load.wait()
    saves = []
    for g in range(half_y // 16):
        at = [pl.ds(g * 16 + 8 * k, 8) for k in range(2)]
        pooled = jnp.concatenate([pooled_ref[:, a, :].reshape(channels * 8, 128) for a in at], 1)
        spectral = jnp.concatenate([spec_ref[:, a, :].reshape(channels * 8, 128) for a in at], 1)
        added = dot_left3(proj_ref[...], gelu(pooled + spectral))
        for k in range(2):
            for b in range(2):
                piece = added[b * channels * 8 : (b + 1) * channels * 8, k * 128 : (k + 1) * 128]
                piece = piece.reshape(channels, 8, 128)
                rows = pl.ds(g * 32 + 16 * k + 8 * b, 8)
                for x in range(local_x):
                    base_ref[:, x, rows, :] += piece
        rows = pl.ds(g * 32, 32)
        save = pltpu.make_async_copy(
            base_ref.at[:, :, rows, :], out_hbm.at[:, :, rows, :], save_sem.at[g]
        )
        save.start()
        saves.append(save)
    for save in saves:
        save.wait()


def on_device(features, fine_weights, middle_weights, lift_fine, lift_middle, project_out):
    channels, local_x, cells_y, cells_z = features.shape
    n = lax.axis_size("gx")
    owned = fine_weights.shape[0]
    owned_c = middle_weights.shape[0]
    half_ky, half_kz = KY // 2, KZ // 2
    narrow = 8
    fits = (
        owned == 3 * KZ
        and KZ == 32
        and KY == 3 * n
        and owned_c % narrow == 0
        and local_x == 2
        and cells_z == 128
        and cells_y % 32 == 0
        and channels % 16 == 0
    )
    if not fits:
        return general_device(
            features, fine_weights, middle_weights, lift_fine, lift_middle, project_out
        )
    modes_x = fine_weights.shape[1]
    modes_c = middle_weights.shape[1]
    tx = np.asarray(host_table(modes_x, local_x * n), np.float32).reshape(modes_x, n, local_x)
    txc = np.asarray(host_table(modes_c, n), np.float32)
    wire = forward_fine(features, KY, KZ, n)
    slab, lifted, liftm, proj, projm = mix_fine(
        wire, fine_weights, features, (lift_fine, lift_middle, project_out), tx, n
    )

    half_y, half_z = cells_y // 2, cells_z // 2
    pool_y = np.repeat(np.eye(half_y), 2, axis=1) * 0.5
    pool_z = np.repeat(np.eye(half_z), 2, axis=1) * 0.25
    ty_c = host_table(half_ky, half_y)
    tz_c = host_table(half_kz, half_z)
    parts = half_kz // narrow
    per_c = 128 // narrow
    chunks_c = channels // per_c
    yc = left_rows(np.concatenate([pool_y, ty_c @ pool_y], 0))
    zc_full = (tz_c @ pool_z).T.reshape(cells_z, parts, 1, narrow)
    zc = right_three(np.broadcast_to(zc_full, (cells_z, parts, per_c, narrow)).reshape(cells_z, -1))
    zp = np.repeat(pool_z, 2, axis=0).T
    zp = np.asarray(zp, jnp.bfloat16)
    zp = jnp.asarray(np.concatenate([zp, zp], 0))
    ty_i = left_three(host_table(KY, cells_y).T)
    tz_i = right_three(np.tile(host_table(KZ, cells_z), (4, 1)))
    level, pooled, coarse = pl.pallas_call(
        middle_kernel,
        out_shape=(
            jax.ShapeDtypeStruct(features.shape, F32),
            jax.ShapeDtypeStruct((channels, half_y, 128), F32),
            jax.ShapeDtypeStruct((half_ky * parts * chunks_c, 128), F32),
        ),
        in_specs=[whole(), far()] + [whole()] * 5,
        out_specs=(far(), whole(), whole()),
        scratch_shapes=[
            pltpu.VMEM(features.shape, F32),
            pltpu.VMEM((channels, cells_y, cells_z), F32),
            pltpu.VMEM((KY * local_x * channels, cells_z), F32),
            pltpu.VMEM(features.shape, F32),
            pltpu.SemaphoreType.DMA((2,)),
        ],
        name="middle",
    )(slab, lifted, ty_i, tz_i, yc, zc, zp)

    count = owned_c // narrow
    rows = count * chunks_c
    modal, base_low = coarse_call(
        coarse_out_kernel, n, txc, rows, 1, ((modes_c, rows, 128),),
        coarse, features, level, proj,
    )
    modal = modal.reshape(modes_c, count, channels, narrow).transpose(1, 3, 0, 2)
    mixed = mix_modes(modal.reshape(owned_c, modes_c, channels), middle_weights)
    mixed = mixed.reshape(count, narrow, modes_c, channels).transpose(2, 0, 3, 1)
    slab, base_high, lifted = coarse_call(
        coarse_back_kernel, n, txc, rows, 2, ((n * rows, 128), pooled.shape),
        mixed.reshape(modes_c, rows, 128), features, level, proj, pooled, liftm,
    )

    tyc_i = left_three(ty_c.T)
    grown = np.repeat(tz_c, 2, axis=1).reshape(parts, 1, narrow, cells_z)
    tzc_i = right_three(np.broadcast_to(grown, (parts, per_c, narrow, cells_z)).reshape(-1, cells_z))
    return pl.pallas_call(
        final_kernel,
        out_shape=jax.ShapeDtypeStruct(features.shape, F32),
        in_specs=[whole(), whole(), far(), far()] + [whole()] * 3,
        out_specs=far(),
        scratch_shapes=[
            pltpu.VMEM((channels, half_y, 128), F32),
            pltpu.VMEM(features.shape, F32),
            pltpu.SemaphoreType.DMA((2,)),
            pltpu.SemaphoreType.DMA((half_y // 16,)),
        ],
        name="final",
    )(slab, lifted, base_low, base_high, tyc_i, tzc_i, projm)


def solution(mesh):
    in_specs = (
        P(None, ("groups", "gx"), None, None),
        P("gx", None, None, None),
        P("gx", None, None, None),
        P(),
        P(),
        P(),
    )
    out_specs = P(None, ("groups", "gx"), None, None)
    return jax.shard_map(
        on_device, mesh=mesh, in_specs=in_specs, out_specs=out_specs, check_vma=False
    )
```
